128 devices in a mesh: gx: 16 (over z, y), gy: 8 (over x, core).
Axes of the slice: x: 4, y: 4, z: 4, core: 2. Of those that a mesh axis runs over, the one named last changes fastest.
Arguments:
- positions: float32 [3, 32768, 128], P(None, ('gx', 'gy')), may hold values from 0 to 1
- masses: float32 [32768, 128], P(('gx', 'gy')), may hold values from 0.004 to 0.012
- smoothing: float32 [32768, 128], P(('gx', 'gy')), may hold values from 0.55 to 1
- entropy: float32 [32768, 128], P(('gx', 'gy')), may hold values from 0.5 to 2
- density: float32 [32768, 128], P(('gx', 'gy')), may hold values from 0.5 to 2
- active_cells: int32 [512], P(('gx', 'gy')), may hold values from 0 to 32767, as said below
- active_count: int32 [128], P(('gx', 'gy')), may hold values from 1 to 4, 324 in all
- neighbours: int32 [512, 27], P(('gx', 'gy')), may hold values from 0 to 32767, as said below
- mig_source: int32 [16384], P(('gx', 'gy')), may hold values from 0 to 32767
- mig_dest: int32 [16384, 1], P(('gx', 'gy')), may hold values from 0 to 127; in each aligned block of 128 rows (0 to 127, 128 to 255, ...) at most 2 rows name the same one
Outputs:
- new_density: float32 [32768, 128], P(('gx', 'gy'))
- acceleration: float32 [3, 512, 128], P(None, ('gx', 'gy'))
- arrivals: float32 [7, 32768], P(None, ('gx', 'gy'))
The draws below stay inside these ranges and needn't reach their ends.
Inputs may be any that keep to these rules, and one draw needn't show every extreme that they name: `active_cells`: the 4 entries of device d are distinct cells of device d. The middle entry (index 13) of a slot is its active cell. Every other entry is a cell of the slot's own device, or a cell of the device just before or just after it in the cell order lying within 64 cells of the end they share. Over all slots of one device, at most 8 distinct cells of each of these two devices are named, and every device with neighbours on both sides names exactly 8 on each side. `mig_dest`: within the 128 rows of one device no destination appears more than 2 times; some destination appears exactly 2 times.
All inputs are finite; a program needn't handle non-finite values. No bound on the sum of `active_count` on one device may be relied on, other than what follows from the above.
Results may differ from the reference program's by a relative error of at most 0.0003.
Values sent between devices are 32-bit elements; how exact they have to be, the bound alone decides.
A program may use at most 64 MiB of HBM per device.

```python
import math
import jax
import jax.numpy as jnp
import numpy as np
from jax import lax

P_SIZE = 128
NBR = 27
CELLS_DEV = 256
MIG_DEV = 128
RIM = 64
ACT_MAX = 4
GHOST_MAX = 8
MIG_CAP = 2
NCELLS = 32768
NACT = 512
NMIG = 16384
N_GX = 16
N_GY = 8


def cell_lists(key):
    devices = N_GX * N_GY
    entries = ACT_MAX * NBR
    device_keys = jax.random.split(jax.random.fold_in(key, 17), devices)

    def ordering_of(one_key):
        return jax.random.permutation(one_key, CELLS_DEV)
    ordering = jax.vmap(ordering_of)(device_keys)
    device_ids = jnp.arange(devices)
    chosen = ordering[:, :ACT_MAX] + (device_ids * CELLS_DEV)[:, None]
    active = chosen.reshape(-1).astype(jnp.int32)
    pool_keys = jax.random.split(jax.random.fold_in(key, 41), devices)

    def left_pool(one_key):
        return jax.random.permutation(one_key, RIM)[:GHOST_MAX]

    def right_pool(one_key):
        return jax.random.permutation(jax.random.fold_in(one_key, 1), RIM)[:GHOST_MAX]
    left_cells = device_ids[:, None] * CELLS_DEV - RIM + jax.vmap(left_pool)(pool_keys)
    right_cells = (device_ids[:, None] + 1) * CELLS_DEV + jax.vmap(right_pool)(pool_keys)
    own_cells = jax.random.randint(jax.random.fold_in(key, 29), (devices, entries), 0, CELLS_DEV) + device_ids[:, None] * CELLS_DEV
    kinds = jax.random.randint(jax.random.fold_in(key, 53), (devices, entries), 0, 4)
    pool_pick = jax.random.randint(jax.random.fold_in(key, 59), (devices, entries), 0, GHOST_MAX)
    flat = jnp.arange(entries)
    column = flat % NBR
    rank = flat - flat // NBR - (column > NBR // 2).astype(jnp.int32)
    forced_left = (rank < GHOST_MAX)[None, :]
    forced_right = jnp.logical_and(rank >= GHOST_MAX, rank < 2 * GHOST_MAX)[None, :]
    kinds = jnp.where(forced_left, 2, jnp.where(forced_right, 3, kinds))
    pool_pick = jnp.where(forced_left, rank[None, :], jnp.where(forced_right, rank[None, :] - GHOST_MAX, pool_pick))
    left_value = jnp.take_along_axis(left_cells, pool_pick, axis=1)
    right_value = jnp.take_along_axis(right_cells, pool_pick, axis=1)
    has_left = (device_ids > 0)[:, None]
    has_right = (device_ids < devices - 1)[:, None]
    picked = jnp.where(jnp.logical_and(kinds == 2, has_left), left_value, jnp.where(jnp.logical_and(kinds == 3, has_right), right_value, own_cells))
    picked = picked.reshape(devices * ACT_MAX, NBR)
    centre = (jnp.arange(NBR) == NBR // 2)[None, :]
    neighbour_ids = jnp.where(centre, active[:, None], picked).astype(jnp.int32)
    return (active, neighbour_ids)


def draw_active_cells(key, part):
    return cell_lists(key)[0]


def draw_neighbours(key, part):
    return cell_lists(key)[1]


def plant(drawn, stream_key, smallest, largest):
    index_at = [jax.random.randint(jax.random.fold_in(stream_key, axis), (), 0, length) for axis, length in enumerate(drawn.shape)]
    main_axis = drawn.shape.index(max(drawn.shape))
    neighbour = index_at[:main_axis] + [(index_at[main_axis] + 1) % drawn.shape[main_axis]] + index_at[main_axis + 1:]
    return drawn.at[tuple(index_at)].set(smallest).at[tuple(neighbour)].set(largest)


def shard_levels(rng, shape, cuts, least, largest):
    def one(dim, shards_of):
        steps = jax.random.uniform(jax.random.fold_in(jax.random.fold_in(rng, 6), dim), (shards_of,), jnp.float32, least / len(cuts), largest / len(cuts))
        return jnp.repeat(jnp.exp(steps), shape[dim] // shards_of).reshape((-1,) + (1,) * (len(shape) - dim - 1))

    gain = one(*cuts[0])
    for cut in cuts[1:]:
        gain = gain * one(*cut)
    return gain


def split_up(number_of, total, reach, skew):
    portions = [(1 << 20) // math.isqrt(rank ** skew) + 1 for rank in range(2, number_of + 1)]
    surplus, given = total - reach - (number_of - 1), [1] * (number_of - 1)
    while surplus > 0:
        candidates = [i for i in range(number_of - 1) if given[i] < reach]
        mass, remaining = sum([portions[i] for i in candidates]), surplus
        for i in candidates:
            addition = min(reach - given[i], max(1, remaining * portions[i] // mass), surplus)
            given[i] = given[i] + addition
            surplus = surplus - addition
    return np.array([reach] + given)


def uneven(key, number_of, total, most, slope):
    if number_of == 2:
        one = jax.random.randint(key, (), max(1, total - most), min(most, total - 1) + 1)
        return jnp.stack([one, total - one])
    sizes = jnp.asarray(split_up(number_of, total, most, slope), jnp.int32)
    pairs = (number_of - 1) // 2
    source_of, sink = sizes[1:1 + 2 * pairs:2], sizes[2:2 + 2 * pairs:2]
    margin = jnp.minimum(source_of - 1, most - sink)
    moved = jax.random.randint(jax.random.fold_in(key, 1), (pairs,), 0, 1 << 20) % (margin + 1)
    sizes = sizes.at[1:1 + 2 * pairs:2].set(source_of - moved).at[2:2 + 2 * pairs:2].set(sink + moved)
    return sizes[jax.random.permutation(jax.random.fold_in(key, 2), number_of)]


def deal_out(key, own, number, rows, count, top, bound, skew):
    order = jax.random.permutation(key, count)
    heavy_load, usual = load_shares(count, rows * top, bound, skew, True), load_shares(count, rows * top, bound, skew, False)
    places = jnp.arange(count)

    def named(tallies, offset_by):
        used = int((tallies > 0).sum())
        fixed = max(1, used // 4)
        shifted = fixed + (places - fixed + offset_by * (used - fixed)) % max(1, count - fixed)
        return jnp.zeros((count,), jnp.int32).at[order[jnp.where(places < fixed, places, shifted)]].set(jnp.asarray(tallies, jnp.int32))

    tallies = jnp.where(number % 4 == 0, named(heavy_load, number // 4), named(usual, number - number // 4 - 1))
    mixed = jax.random.permutation(jax.random.fold_in(own, 3), count)
    source_of, sink = mixed[0:count // 2 * 2:2], mixed[1:count // 2 * 2:2]
    room = jnp.minimum(tallies[source_of] - 1, bound - tallies[sink]) // 2
    room = jnp.where((source_of == order[0]) | (sink == order[0]) | (tallies[sink] == 0), 0, jnp.maximum(room, 0))
    shifted = jax.random.randint(jax.random.fold_in(own, 4), (count // 2,), 0, 1 << 20) % (room + 1)
    tallies = tallies.at[source_of].add(-shifted).at[sink].add(shifted)
    items = jnp.searchsorted(jnp.cumsum(tallies), jnp.arange(rows * top), side="right").astype(jnp.int32)
    grid = items.reshape(top, rows).T
    grid = grid[jax.random.permutation(jax.random.fold_in(own, 1), rows)]
    offset_by = jax.random.randint(jax.random.fold_in(own, 2), (rows, 1), 0, top)
    return jnp.take_along_axis(grid, (jnp.arange(top)[None, :] + offset_by) % top, axis=1)


def load_shares(number_of, total, most, lean, full):
    portions = [(1 << 20) // math.isqrt(rank ** lean) + 1 for rank in range(1, number_of + 1)]
    largest = most if full else min(most, max(-(-total // number_of), total * portions[0] // sum(portions)))
    least = 1 if total - largest >= number_of - 1 else 0
    holding, rest = [largest] + [least] * (number_of - 1), total - largest - least * (number_of - 1)
    while rest > 0:
        movable = [i for i in range(1, number_of) if holding[i] < largest] or [i for i in range(1, number_of) if holding[i] < most]
        whole, budget = sum([portions[i] for i in movable]), rest
        for i in movable:
            extra = min(most - holding[i], max(1, budget * portions[i] // whole), rest)
            holding[i] = holding[i] + extra
            rest = rest - extra
    return np.array(holding)


def setup_inputs(seed: int = 0) -> dict:
    splits = jax.random.split(jax.random.key(seed), 11)
    positions = jnp.clip(1.0 * jax.random.uniform(splits[0], (3, NCELLS, P_SIZE), jnp.float32) ** shard_levels(splits[0], (3, NCELLS, P_SIZE), ((1, 128),), -0.2, 0.2), 0.0, 1.0)
    masses = jnp.clip(jnp.exp(math.log(0.012) - 1.09861225 * jax.random.uniform(splits[1], (NCELLS, P_SIZE), jnp.float32) ** shard_levels(splits[1], (NCELLS, P_SIZE), ((0, 128),), -0.2, 0.2)), 0.004, 0.012)
    smoothing = jnp.clip(0.55 + 0.45 * jax.random.uniform(splits[2], (NCELLS, P_SIZE), jnp.float32) ** shard_levels(splits[2], (NCELLS, P_SIZE), ((0, 128),), -0.2, 0.2), 0.55, 1.0)
    entropy = jnp.clip(jnp.exp(math.log(2.0) - 1.3862944 * jax.random.uniform(splits[3], (NCELLS, P_SIZE), jnp.float32) ** shard_levels(splits[3], (NCELLS, P_SIZE), ((0, 128),), -0.2, 0.2)), 0.5, 2.0)
    density = jnp.clip(jnp.exp(math.log(2.0) - 1.3862944 * jax.random.uniform(splits[4], (NCELLS, P_SIZE), jnp.float32) ** shard_levels(splits[4], (NCELLS, P_SIZE), ((0, 128),), -0.2, 0.2)), 0.5, 2.0)
    active_cells = draw_active_cells(jax.random.fold_in(splits[10], 71), 0)
    active_count = uneven(splits[6], N_GX * N_GY, N_GX * N_GY * (ACT_MAX + 1) // 2 + ACT_MAX, ACT_MAX, 2).astype(jnp.int32)
    neighbours = draw_neighbours(jax.random.fold_in(splits[10], 71), 0)
    mig_source = plant(jax.random.randint(splits[8], (NMIG,), 0, CELLS_DEV * P_SIZE), jax.random.fold_in(splits[8], 1), 0, (CELLS_DEV * P_SIZE) - 1).astype(jnp.int32)
    mig_dest_keys = jax.random.split(jax.random.fold_in(splits[9], 1), NMIG // MIG_DEV)
    mig_dest_turns = jax.random.permutation(jax.random.fold_in(splits[9], 3), NMIG // MIG_DEV)
    mig_dest = jax.vmap(lambda own, number: deal_out(jax.random.fold_in(splits[9], 2), own, number, MIG_DEV, N_GX * N_GY, 1, MIG_CAP, 2))(mig_dest_keys, mig_dest_turns).reshape((NMIG, 1))
    return {"positions": positions, "masses": masses, "smoothing": smoothing, "entropy": entropy, "density": density, "active_cells": active_cells, "active_count": active_count, "neighbours": neighbours, "mig_source": mig_source, "mig_dest": mig_dest}


kernel_norm = 8.0 / math.pi

def stencil_offsets():
    index = jnp.arange(NBR)
    return jnp.stack([index // 9 - 1, index // 3 % 3 - 1, index % 3 - 1]).astype(jnp.float32)

def kernel_value(ratio):
    inner = 1.0 - 6.0 * ratio * ratio + 6.0 * ratio * ratio * ratio
    outer = 2.0 * (1.0 - ratio) ** 3
    return jnp.where(ratio < 0.5, inner, jnp.where(ratio < 1.0, outer, 0.0))

def kernel_slope(ratio):
    safe_ratio = jnp.maximum(ratio, 0.5)
    inner = -12.0 + 18.0 * ratio
    outer = -6.0 * (1.0 - ratio) ** 2 / safe_ratio
    return jnp.where(ratio < 0.5, inner, jnp.where(ratio < 1.0, outer, 0.0))

def pair_geometry(own_pos, other_pos):
    separation = own_pos[:, :, None, None] - other_pos[:, None, :, :]
    distance = jnp.sqrt(lax.optimization_barrier(jnp.sum(separation * separation, axis=0)))
    return (separation, distance)

def density_cell(own_pos, own_len, other_pos, other_mass):
    separation, distance = pair_geometry(own_pos, other_pos)
    weights = kernel_value(distance / own_len[:, None, None])
    return kernel_norm * lax.optimization_barrier(jnp.sum(other_mass[None] * weights, axis=(1, 2))) / own_len ** 3

def force_cell(own_pos, own_len, own_rho, own_press, other_pos, other_mass, other_len, other_rho, other_press):
    separation, distance = pair_geometry(own_pos, other_pos)
    own_term = (own_press / own_rho ** 2 * kernel_norm / own_len ** 5)[:, None, None] * kernel_slope(distance / own_len[:, None, None])
    other_term = (other_press / other_rho ** 2 * kernel_norm / other_len ** 5)[None] * kernel_slope(distance / other_len[None])
    factor = other_mass[None] * (own_term + other_term)
    return -lax.optimization_barrier(jnp.sum(factor[None] * separation, axis=(2, 3)))

def reference(positions, masses, smoothing, entropy, density, active_cells, active_count, neighbours, mig_source, mig_dest):
    devices = N_GX * N_GY
    stencil = stencil_offsets()
    live_slot = jnp.arange(NACT) % ACT_MAX < jnp.repeat(active_count, ACT_MAX)

    def density_one(inputs):
        cell, near_ids = inputs
        other_pos = positions[:, near_ids, :] + stencil[:, :, None]
        return density_cell(positions[:, cell, :], smoothing[cell], other_pos, masses[near_ids])
    rho = lax.map(density_one, (active_cells, neighbours))
    kept = jnp.where(live_slot[:, None], rho, density[active_cells])
    new_density = density.at[active_cells].set(kept)
    pressure = entropy * jnp.exp(5.0 / 3.0 * jnp.log(new_density))

    def force_one(inputs):
        cell, near_ids = inputs
        other_pos = positions[:, near_ids, :] + stencil[:, :, None]
        return force_cell(positions[:, cell, :], smoothing[cell], new_density[cell], pressure[cell], other_pos, masses[near_ids], smoothing[near_ids], new_density[near_ids], pressure[near_ids])
    accel_rows = lax.map(force_one, (active_cells, neighbours))
    acceleration = jnp.transpose(accel_rows, (1, 0, 2)) * live_slot[None, :, None].astype(jnp.float32)
    source_dev = (jnp.arange(NMIG) // MIG_DEV).astype(jnp.int32)
    cell_ids = (source_dev * CELLS_DEV + mig_source // P_SIZE).astype(jnp.int32)
    lane_ids = (mig_source % P_SIZE).astype(jnp.int32)
    state = jnp.concatenate([positions[:, cell_ids, lane_ids], masses[cell_ids, lane_ids][None], smoothing[cell_ids, lane_ids][None], entropy[cell_ids, lane_ids][None], new_density[cell_ids, lane_ids][None]], axis=0)
    destination = mig_dest[:, 0].reshape(devices, MIG_DEV)
    same = destination[:, :, None] == destination[:, None, :]
    earlier = jnp.arange(MIG_DEV)[None, :] < jnp.arange(MIG_DEV)[:, None]
    slot_rank = lax.optimization_barrier(jnp.sum(jnp.logical_and(same, earlier[None]), axis=2)).astype(jnp.int32).reshape(-1)
    column = (mig_dest[:, 0] * devices * MIG_CAP + source_dev * MIG_CAP + slot_rank).astype(jnp.int32)
    arrivals = jnp.zeros((7, devices * devices * MIG_CAP), jnp.float32).at[:, column].set(state)
    return (new_density, acceleration, arrivals)
```

```python
import functools
import math

import jax
import jax.numpy as jnp
from jax import lax
from jax.experimental import pallas as pl
from jax.experimental.pallas import tpu as pltpu
from jax.sharding import PartitionSpec as P

CELLS = 256
LANES = 128
RIM = 64
EXT = CELLS + 2 * RIM
NBR = 27
PAD = 32
SLOTS = 4
ROWS = 128
NORM = 8.0 / math.pi
TINY = 1e-12
UNROLL = 27

F32 = jnp.float32
BF16 = jnp.bfloat16
MESH = pl.DeviceIdType.MESH
NT = (((1,), (1,)), ((), ()))
NN = (((1,), (0,)), ((), ()))


def dot(a, b, dims=NN):
    return lax.dot_general(a, b, dims, preferred_element_type=F32)


def parts(value, count):
    out = []
    for _ in range(count - 1):
        head = value.astype(BF16).astype(F32)
        out.append(head)
        value = value - head
    out.append(value.astype(BF16).astype(F32))
    return out


def exact(select, value, dims=NN):
    return sum(dot(select, part.astype(BF16), dims) for part in parts(value, 3))


def iota(shape, dim):
    return lax.broadcasted_iota(jnp.int32, shape, dim)


def kernel(
    n_gx,
    n_gy,
    act,
    cnt,
    nbr,
    src,
    pos,
    mas,
    smo,
    ent,
    den,
    src_row,
    dst_row,
    nbr_mat,
    o_den,
    o_acc,
    o_arr,
    own,
    ext,
    tiles,
    bpart,
    mtile,
    ai,
    aj,
    idt,
    rho,
    outb,
    st1,
    st2,
    st3,
    load_sem,
    rim_send,
    rim_recv,
    id_send,
    id_recv,
    rho_send,
    rho_recv,
    a_send,
    a_recv,
    b_send,
    b_recv,
):
    gx, gy = lax.axis_index("gx"), lax.axis_index("gy")
    n_dev = n_gx * n_gy
    me = gx * n_gy + gy
    prev, nxt = (me + n_dev - 1) % n_dev, (me + 1) % n_dev
    near = [(prev // n_gy, prev % n_gy), (nxt // n_gy, nxt % n_gy)]

    barrier = pltpu.get_barrier_semaphore()
    for target in near:
        pl.semaphore_signal(barrier, inc=1, device_id=target, device_id_type=MESH)
    for k in range(1, n_gy):
        pl.semaphore_signal(
            barrier, inc=1, device_id=(gx, (gy + k) % n_gy), device_id_type=MESH
        )
    for k in range(1, n_gx):
        pl.semaphore_signal(
            barrier, inc=1, device_id=((gx + k) % n_gx, gy), device_id_type=MESH
        )

    fields = [pos.at[0], pos.at[1], pos.at[2], mas, smo, ent, den]
    loads = [
        pltpu.make_async_copy(f, own.at[pl.ds(v * CELLS, CELLS)], load_sem.at[0, v])
        for v, f in enumerate(fields)
    ]
    fills = [
        pltpu.make_async_copy(f, ext.at[pl.ds(v * EXT + RIM, CELLS)], load_sem.at[1, v])
        for v, f in enumerate(fields)
    ]
    for copy in loads + fills:
        copy.start()

    base = me * CELLS
    sub8 = iota((8, LANES), 0)
    ids = jnp.full((8, LANES), -1, jnp.int32)
    for s in range(SLOTS):
        ids = jnp.where((sub8 == s) & (s < cnt[0]), act[s], ids)
    idt[0] = ids.astype(F32)
    ext[pl.ds(7 * EXT, EXT), :] = jnp.zeros((EXT, LANES), F32)
    own[pl.ds(7 * CELLS, CELLS), :] = jnp.zeros((CELLS, LANES), F32)

    dest = dst_row[...]
    place = (dest % n_gy) * n_gx + dest // n_gy
    to_dest = (iota((LANES, ROWS), 0) == place).astype(F32)
    earlier = (iota((ROWS, ROWS), 0) < iota((ROWS, ROWS), 1)).astype(F32)
    before = dot(to_dest.astype(BF16), earlier.astype(BF16))
    rank = jnp.sum(to_dest * before, axis=0, keepdims=True)
    to_dest = to_dest.astype(BF16)
    src_cell = src_row[...] // LANES
    src_lane = src_row[...] % LANES
    pick_lane = (iota((LANES, ROWS), 0) == src_lane).astype(F32).astype(BF16)
    from_slot = ((src_cell + base).astype(F32) == idt[0]).astype(F32)
    is_new = jnp.sum(from_slot, axis=0, keepdims=True)

    for copy in loads:
        copy.wait()

    lane8 = iota((8, LANES), 1)

    def mig_row(r, state):
        where_from = src[r]
        tile = own[pl.ds(where_from // LANES, 8, stride=CELLS), :]
        value = jnp.sum(
            jnp.where(lane8 == where_from % LANES, tile, 0.0), axis=1, keepdims=True
        )
        return jnp.where(lane8 == r, value, state)

    state = lax.fori_loop(0, ROWS, mig_row, jnp.zeros((8, LANES), F32), unroll=8)

    pl.semaphore_wait(barrier, 2 + n_gy - 1 + n_gx - 1)

    sends = []
    for side, target in enumerate(near):
        first = 0 if side == 0 else CELLS - RIM
        land = RIM + CELLS if side == 0 else 0
        for v, f in enumerate(fields):
            sends.append(
                pltpu.make_async_remote_copy(
                    src_ref=f.at[pl.ds(first, RIM)],
                    dst_ref=ext.at[pl.ds(v * EXT + land, RIM)],
                    send_sem=rim_send.at[side, v],
                    recv_sem=rim_recv.at[side, v],
                    device_id=target,
                    device_id_type=MESH,
                )
            )
        sends.append(
            pltpu.make_async_remote_copy(
                src_ref=idt.at[0],
                dst_ref=idt.at[2 - side],
                send_sem=id_send.at[side],
                recv_sem=id_recv.at[side],
                device_id=target,
                device_id_type=MESH,
            )
        )
    for copy in sends:
        copy.start()
    for copy in fills + sends:
        copy.wait()

    for s in range(SLOTS):
        def fetch(k, _, s=s):
            cell = jnp.clip(nbr[s, k] - (base - RIM), 0, EXT - 1)
            row = pl.multiple_of((s * PAD + k) * 8, 8)
            tiles[pl.ds(row, 8), :] = ext[pl.ds(cell, 8, stride=EXT), :]
            return 0

        lax.fori_loop(0, NBR, fetch, 0, unroll=9)
        tiles[(s * PAD + NBR) * 8 : (s + 1) * PAD * 8, :] = jnp.ones(
            ((PAD - NBR) * 8, LANES), F32
        )

    entries = SLOTS * PAD

    def field(v):
        return tiles[pl.ds(v, entries, stride=8), :]

    k_of = iota((entries, LANES), 0) % PAD
    offset = [k_of // 9 - 1, (k_of // 3) % 3 - 1, k_of % 3 - 1]
    x = [field(v) - 0.5 + offset[v].astype(F32) for v in range(3)]
    mass = field(3)
    length = field(4)
    inv_len = 1.0 / length
    inv2 = inv_len * inv_len
    n2 = x[0] * x[0] + x[1] * x[1] + x[2] * x[2]

    def put_b(values):
        for c, value in enumerate(values):
            for p, part in enumerate(parts(value, 3)):
                bpart[pl.ds(p * 8 + c, entries, stride=24), :] = part

    def put_m(values):
        for c, value in enumerate(values):
            for p, part in enumerate(parts(value, 2)):
                mtile[pl.ds(p * 8 + c, entries, stride=16), :] = part

    one = jnp.ones((entries, LANES), F32)
    bpart[...] = jnp.zeros_like(bpart)
    mtile[...] = jnp.zeros_like(mtile)
    put_b([x[0], x[1], x[2], n2, one])
    put_m([mass * x[0], mass * x[1], mass * x[2], mass])

    def mid(value, s):
        return value[s * PAD + NBR // 2 : s * PAD + NBR // 2 + 1, :]

    own_x, own_inv, own_len = [], [], []
    zero3 = jnp.zeros((3, LANES), F32)
    for s in range(SLOTS):
        xs = [mid(x[v], s) for v in range(3)]
        hi2, ns = mid(inv2, s), mid(n2, s)
        own_x.append(jnp.concatenate(xs + [jnp.zeros((5, LANES), F32)], axis=0))
        own_inv.append(mid(inv_len, s))
        scaled = jnp.concatenate([-2.0 * hi2 * v for v in xs] + [hi2, hi2 * ns, zero3], axis=0)
        plain = jnp.concatenate(
            [-2.0 * v for v in xs] + [jnp.ones((1, LANES), F32), ns, zero3], axis=0
        )
        for ref, tile in ((ai, scaled), (aj, plain)):
            h, m, l = parts(tile, 3)
            big = jnp.concatenate([h, h, m, m, h, l, jnp.zeros((80, LANES), F32)], axis=0)
            ref[s] = jnp.transpose(big).astype(BF16)

    def pair_pass(a_ref, function, terms):
        def slot(s):
            a = a_ref[s][:, :48]
            total = jnp.zeros((16, LANES), F32)
            for k in range(NBR):
                e = s * PAD + k
                t = bpart[e * 24 : e * 24 + 24, :]
                h, m, l = t[0:8], t[8:16], t[16:24]
                b = jnp.concatenate([h, m, h, m, l, h], axis=0).astype(BF16)
                q2 = jnp.maximum(dot(a, b), TINY)
                value = function(q2)
                lhs = mtile[e * 16 : e * 16 + 16, :].astype(BF16)
                high = value.astype(BF16)
                total += dot(lhs, high, NT)
                if terms == 2:
                    total += dot(lhs, (value - high.astype(F32)).astype(BF16), NT)
            return total[0:8] + total[8:16]

        return [slot(s) for s in range(SLOTS)]

    def weight(q2):
        q = q2 * lax.rsqrt(q2)
        u = jnp.maximum(1.0 - q, 0.0)
        v = jnp.maximum(u - q, 0.0)
        return (u + u) * (u * u) - v * (v * v)

    def slope(q2):
        inv_q = lax.rsqrt(q2)
        q = q2 * inv_q
        u = 1.0 - q
        v = jnp.maximum(u - q, 0.0)
        return jnp.minimum(jnp.maximum(inv_q - 1.0, 0.0), 1.0) * (u + v)

    sums = pair_pass(ai, weight, 2)
    rho_rows = []
    for s in range(SLOTS):
        rho_rows.append(NORM * sums[s][3:4] * own_inv[s] * own_inv[s] * own_inv[s])
    rho8 = jnp.concatenate(rho_rows + [jnp.ones((4, LANES), F32)], axis=0)
    rho[0] = rho8

    moved = jnp.sum(from_slot * exact_rows(rho8, pick_lane), axis=0, keepdims=True)
    fresh = jnp.where(is_new > 0.5, moved, state[6:7])
    full = jnp.where(sub8 == 6, fresh, state)
    ranked = jnp.concatenate(
        [
            jnp.where(rank < 0.5, full, 0.0),
            jnp.where(rank < 0.5, 0.0, full),
            jnp.zeros((112, LANES), F32),
        ],
        axis=0,
    )
    outb[...] = exact(to_dest, ranked, NT)

    rho_copies = [
        pltpu.make_async_remote_copy(
            src_ref=rho.at[0],
            dst_ref=rho.at[2 - side],
            send_sem=rho_send.at[side],
            recv_sem=rho_recv.at[side],
            device_id=target,
            device_id_type=MESH,
        )
        for side, target in enumerate(near)
    ]
    for copy in rho_copies:
        copy.start()
    first_stage = []
    for k in range(1, n_gy):
        other = (gy + k) % n_gy
        first_stage.append(
            pltpu.make_async_remote_copy(
                src_ref=outb.at[pl.ds(pl.multiple_of(other * n_gx, n_gx), n_gx)],
                dst_ref=st1.at[pl.ds(pl.multiple_of(gy * n_gx, n_gx), n_gx)],
                send_sem=a_send.at[k],
                recv_sem=a_recv.at[k],
                device_id=(gx, other),
                device_id_type=MESH,
            )
        )
    for copy in first_stage:
        copy.start()
    mine = pl.ds(pl.multiple_of(gy * n_gx, n_gx), n_gx)
    st1[mine, :] = outb[mine, :]

    table = ext[6 * EXT + RIM : 6 * EXT + RIM + CELLS, :]
    row_id = iota((CELLS, LANES), 0)
    for s in range(SLOTS):
        hit = (row_id == act[s] - base) & (s < cnt[0])
        table = jnp.where(hit, rho8[s : s + 1], table)
    o_den[...] = table

    own_force = pair_pass(ai, slope, 2)

    for copy in first_stage:
        copy.wait()
    for a in range(n_gx):
        st2[a * n_gy : (a + 1) * n_gy, :] = st1[pl.ds(a, n_gy, stride=n_gx), :]
    second_stage = []
    for k in range(1, n_gx):
        other = (gx + k) % n_gx
        second_stage.append(
            pltpu.make_async_remote_copy(
                src_ref=st2.at[pl.ds(pl.multiple_of(other * n_gy, n_gy), n_gy)],
                dst_ref=st3.at[pl.ds(pl.multiple_of(gx * n_gy, n_gy), n_gy)],
                send_sem=b_send.at[k],
                recv_sem=b_recv.at[k],
                device_id=(other, gy),
                device_id_type=MESH,
            )
        )
    for copy in second_stage:
        copy.start()
    mine = pl.ds(pl.multiple_of(gx * n_gy, n_gy), n_gy)
    st3[mine, :] = st2[mine, :]

    for copy in rho_copies:
        copy.wait()

    candidates = jnp.concatenate([idt[0], idt[1], idt[2]], axis=0)
    wanted = jnp.full((1, LANES), -2, jnp.int32)
    lane1 = iota((1, LANES), 1)
    spread = jnp.concatenate(
        [nbr_mat[...], jnp.zeros((SLOTS, LANES - NBR), jnp.int32)], axis=1
    )
    for s in range(SLOTS):
        line = spread[s : s + 1]
        if s:
            line = pltpu.roll(line, s * PAD, 1)
        wanted = jnp.where((lane1 >= s * PAD) & (lane1 < s * PAD + NBR), line, wanted)
    match = (candidates == wanted.astype(F32)).astype(F32)
    match = jnp.transpose(jnp.concatenate([match, jnp.zeros((104, LANES), F32)], axis=0))
    news = jnp.concatenate([rho[0], rho[1], rho[2], jnp.zeros((104, LANES), F32)], axis=0)
    patch = exact(match.astype(BF16), news)
    hits = jnp.sum(match, axis=1, keepdims=True)
    dens = jnp.where(hits > 0.5, patch, field(6))
    inv4 = inv2 * inv2
    factor = mass * field(5) * jnp.exp(jnp.log(dens) * (-1.0 / 3.0)) * (inv4 * inv_len)
    put_b([x[0] * inv2, x[1] * inv2, x[2] * inv2, n2 * inv2, inv2])
    put_m([factor * x[0], factor * x[1], factor * x[2], factor])

    other_force = pair_pass(aj, slope, 2)

    live = cnt[0]
    for s in range(SLOTS):
        own_s = sums_of(own_force[s], own_x[s])
        other_s = sums_of(other_force[s], own_x[s])
        entropy_i = mid(field(5), s)
        rho_i = mid(dens, s)
        front = entropy_i * jnp.exp(jnp.log(rho_i) * (-1.0 / 3.0))
        front = front * (mid(inv4, s) * own_inv[s])
        result = (6.0 * NORM) * (front * own_s + other_s)
        result = jnp.where(s < live, result, 0.0)
        o_acc[:, s, :] = result[0:3]

    for copy in second_stage:
        copy.wait()
    turned = jnp.transpose(st3[...])
    halves = jnp.concatenate([turned[0:8], turned[8:16]], axis=1)
    width = 2 * n_dev
    source = iota((2 * LANES, width), 0)
    column = iota((2 * LANES, width), 1)
    spot = (source % LANES) * 2 + source // LANES
    o_arr[...] = sum(
        dot(part.astype(BF16), (spot == column).astype(F32).astype(BF16))
        for part in parts(halves, 3)
    )[0:7]


def exact_rows(value, select):
    return sum(dot(part.astype(BF16), select) for part in parts(value, 3))


def sums_of(total, own_x):
    return own_x * total[3:4] - total


def local(
    n_gx,
    n_gy,
    positions,
    masses,
    smoothing,
    entropy,
    density,
    active_cells,
    active_count,
    neighbours,
    mig_source,
    mig_dest,
):
    smem = pl.BlockSpec(memory_space=pltpu.SMEM)
    vmem = pl.BlockSpec(memory_space=pltpu.VMEM)
    hbm = pl.BlockSpec(memory_space=pl.ANY)
    n_dev = n_gx * n_gy
    entries = SLOTS * PAD
    dma = pltpu.SemaphoreType.DMA
    return pl.pallas_call(
        functools.partial(kernel, n_gx, n_gy),
        out_shape=(
            jax.ShapeDtypeStruct((CELLS, LANES), F32),
            jax.ShapeDtypeStruct((3, SLOTS, LANES), F32),
            jax.ShapeDtypeStruct((7, 2 * n_dev), F32),
        ),
        in_specs=[smem] * 4 + [hbm] * 5 + [vmem] * 3,
        out_specs=(vmem, vmem, vmem),
        scratch_shapes=[
            pltpu.VMEM((8 * CELLS, LANES), F32),
            pltpu.VMEM((8 * EXT, LANES), F32),
            pltpu.VMEM((entries * 8, LANES), F32),
            pltpu.VMEM((entries * 24, LANES), F32),
            pltpu.VMEM((entries * 16, LANES), F32),
            pltpu.VMEM((SLOTS, LANES, LANES), BF16),
            pltpu.VMEM((SLOTS, LANES, LANES), BF16),
            pltpu.VMEM((3, 8, LANES), F32),
            pltpu.VMEM((3, 8, LANES), F32),
            pltpu.VMEM((LANES, LANES), F32),
            pltpu.VMEM((LANES, LANES), F32),
            pltpu.VMEM((LANES, LANES), F32),
            pltpu.VMEM((LANES, LANES), F32),
            dma((2, 7)),
            dma((2, 7)),
            dma((2, 7)),
            dma((2,)),
            dma((2,)),
            dma((2,)),
            dma((2,)),
            dma((n_gy,)),
            dma((n_gy,)),
            dma((n_gx,)),
            dma((n_gx,)),
        ],
        compiler_params=pltpu.CompilerParams(collective_id=0, has_side_effects=True),
    )(
        active_cells,
        active_count,
        neighbours,
        mig_source,
        positions,
        masses,
        smoothing,
        entropy,
        density,
        mig_source.reshape(1, ROWS),
        mig_dest.reshape(1, ROWS),
        neighbours,
    )


def solution(mesh):
    both = ("gx", "gy")
    placed = (
        P(None, both, None),
        P(both, None),
        P(both, None),
        P(both, None),
        P(both, None),
        P(both),
        P(both),
        P(both, None),
        P(both),
        P(both, None),
    )
    return jax.shard_map(
        functools.partial(local, mesh.shape["gx"], mesh.shape["gy"]),
        mesh=mesh,
        in_specs=placed,
        out_specs=(P(both, None), P(None, both, None), P(None, both)),
        check_vma=False,
    )
```

```python
import functools
import math

import jax
import jax.numpy as jnp
from jax import lax
from jax.experimental import pallas as pl
from jax.experimental.pallas import tpu as pltpu
from jax.sharding import PartitionSpec as P

CELLS = 256
LANES = 128
RIM = 64
EXT = CELLS + 2 * RIM
NBR = 27
PAD = 32
SLOTS = 4
ROWS = 128
NORM = 8.0 / math.pi
TINY = 1e-12
CHUNK = 32

F32 = jnp.float32
BF16 = jnp.bfloat16
MESH = pl.DeviceIdType.MESH
NT = (((1,), (1,)), ((), ()))
NN = (((1,), (0,)), ((), ()))


def dot(a, b, dims=NN):
    return lax.dot_general(a, b, dims, preferred_element_type=F32)


def parts(value, count):
    out = []
    for _ in range(count - 1):
        head = value.astype(BF16).astype(F32)
        out.append(head)
        value = value - head
    out.append(value.astype(BF16).astype(F32))
    return out


def exact(select, value, dims=NN):
    return sum(dot(select, part.astype(BF16), dims) for part in parts(value, 3))


def iota(shape, dim):
    return lax.broadcasted_iota(jnp.int32, shape, dim)


def kernel(
    n_gx,
    n_gy,
    act,
    cnt,
    nbr,
    src,
    pos,
    mas,
    smo,
    ent,
    den,
    src_row,
    dst_row,
    nbr_mat,
    o_rho,
    o_acc,
    o_arr,
    own,
    ext,
    ext2,
    tiles,
    tiles2,
    bpart,
    mtile,
    ab,
    sq,
    hi_part,
    lo_part,
    acc,
    idt,
    rho,
    outb,
    st1,
    st2,
    st3,
    load_sem,
    rim_send,
    rim_recv,
    id_send,
    id_recv,
    rho_send,
    rho_recv,
    a_send,
    a_recv,
    b_send,
    b_recv,
):
    gx, gy = lax.axis_index("gx"), lax.axis_index("gy")
    n_dev = n_gx * n_gy
    me = gx * n_gy + gy
    prev, nxt = (me + n_dev - 1) % n_dev, (me + 1) % n_dev
    near = [(prev // n_gy, prev % n_gy), (nxt // n_gy, nxt % n_gy)]

    barrier = pltpu.get_barrier_semaphore()
    for target in near:
        pl.semaphore_signal(barrier, inc=1, device_id=target, device_id_type=MESH)
    for k in range(1, n_gy):
        pl.semaphore_signal(
            barrier, inc=1, device_id=(gx, (gy + k) % n_gy), device_id_type=MESH
        )
    for k in range(1, n_gx):
        pl.semaphore_signal(
            barrier, inc=1, device_id=((gx + k) % n_gx, gy), device_id_type=MESH
        )

    fields = [pos.at[0], pos.at[1], pos.at[2], mas, smo, ent, den]

    def place_of(v, row, rows):
        if v < 4:
            return ext.at[pl.ds(v * EXT + row, rows)]
        return ext2.at[pl.ds((v - 4) * EXT + row, rows)]

    loads = [
        pltpu.make_async_copy(f, own.at[pl.ds(v * CELLS, CELLS)], load_sem.at[0, v])
        for v, f in enumerate(fields)
    ]
    fills = [
        pltpu.make_async_copy(f, place_of(v, RIM, CELLS), load_sem.at[1, v])
        for v, f in enumerate(fields)
    ]
    for copy in loads + fills:
        copy.start()

    base = me * CELLS
    sub8 = iota((8, LANES), 0)
    ids = jnp.full((8, LANES), -1, jnp.int32)
    for s in range(SLOTS):
        ids = jnp.where((sub8 == s) & (s < cnt[0]), act[s], ids)
    idt[0] = ids.astype(F32)
    ext2[pl.ds(3 * EXT, EXT), :] = jnp.zeros((EXT, LANES), F32)
    own[pl.ds(7 * CELLS, CELLS), :] = jnp.zeros((CELLS, LANES), F32)

    dest = dst_row[...]
    place = (dest % n_gy) * n_gx + dest // n_gy
    to_dest = (iota((LANES, ROWS), 0) == place).astype(F32)
    earlier = (iota((ROWS, ROWS), 0) < iota((ROWS, ROWS), 1)).astype(F32)
    before = dot(to_dest.astype(BF16), earlier.astype(BF16))
    rank = jnp.sum(to_dest * before, axis=0, keepdims=True)
    to_dest = to_dest.astype(BF16)
    src_cell = src_row[...] // LANES
    src_lane = src_row[...] % LANES
    pick_lane = (iota((LANES, ROWS), 0) == src_lane).astype(F32).astype(BF16)
    from_slot = ((src_cell + base).astype(F32) == idt[0]).astype(F32)
    is_new = jnp.sum(from_slot, axis=0, keepdims=True)

    for copy in loads:
        copy.wait()

    lane8 = iota((8, LANES), 1)

    def mig_row(r, state):
        where_from = src[r]
        tile = own[pl.ds(where_from // LANES, 8, stride=CELLS), :]
        value = jnp.sum(
            jnp.where(lane8 == where_from % LANES, tile, 0.0), axis=1, keepdims=True
        )
        return jnp.where(lane8 == r, value, state)

    state = lax.fori_loop(0, ROWS, mig_row, jnp.zeros((8, LANES), F32), unroll=8)
    own_len = []
    for s in range(SLOTS):
        row = jnp.clip(act[s] - base, 0, CELLS - 1)
        own_len.append(own[pl.ds(row + 4 * CELLS, 1), :])
    for s in range(SLOTS):
        for t in (tiles, tiles2):
            t[(s * PAD + NBR) * 4 : (s + 1) * PAD * 4, :] = jnp.ones(
                ((PAD - NBR) * 4, LANES), F32
            )
    bpart[...] = jnp.zeros_like(bpart)
    mtile[...] = jnp.zeros_like(mtile)

    pl.semaphore_wait(barrier, 2 + n_gy - 1 + n_gx - 1)

    def rim(side, v):
        first = 0 if side == 0 else CELLS - RIM
        land = RIM + CELLS if side == 0 else 0
        return pltpu.make_async_remote_copy(
            src_ref=fields[v].at[pl.ds(first, RIM)],
            dst_ref=place_of(v, land, RIM),
            send_sem=rim_send.at[side, v],
            recv_sem=rim_recv.at[side, v],
            device_id=near[side],
            device_id_type=MESH,
        )

    early = [rim(side, v) for v in range(4) for side in range(2)]
    late = [rim(side, v) for v in range(4, 7) for side in range(2)]
    for side, target in enumerate(near):
        late.append(
            pltpu.make_async_remote_copy(
                src_ref=idt.at[0],
                dst_ref=idt.at[2 - side],
                send_sem=id_send.at[side],
                recv_sem=id_recv.at[side],
                device_id=target,
                device_id_type=MESH,
            )
        )
    for copy in early + late:
        copy.start()
    for copy in fills + early:
        copy.wait()

    def gather(into, out_of):
        for s in range(SLOTS):
            def fetch(k, _, s=s):
                cell = jnp.clip(nbr[s, k] - (base - RIM), 0, EXT - 1)
                into[pl.ds((s * PAD + k) * 4, 4), :] = out_of[pl.ds(cell, 4, stride=EXT), :]
                return 0

            lax.fori_loop(0, NBR, fetch, 0, unroll=9)

    entries = SLOTS * PAD
    gather(tiles, ext)
    k_of = iota((entries, LANES), 0) % PAD
    offset = [k_of // 9 - 1, (k_of // 3) % 3 - 1, k_of % 3 - 1]

    def field(v):
        ref = tiles if v < 4 else tiles2
        return ref[pl.ds(v % 4, entries, stride=4), :]

    x = [field(v) - 0.5 + offset[v].astype(F32) for v in range(3)]
    mass = field(3)
    n2 = x[0] * x[0] + x[1] * x[1] + x[2] * x[2]

    def put_b(at, values):
        for c, value in enumerate(values):
            for p, part in enumerate(parts(value, 3)):
                bpart[pl.ds(at * entries * 24 + p * 8 + c, entries, stride=24), :] = part

    def put_m(values):
        for c, value in enumerate(values):
            for p, part in enumerate(parts(value, 2)):
                mtile[pl.ds(p * 8 + c, entries, stride=16), :] = part

    one = jnp.ones((entries, LANES), F32)
    put_b(0, [x[0], x[1], x[2], n2, one])
    put_m([mass * x[0], mass * x[1], mass * x[2], mass])

    def mid(value, s):
        return value[s * PAD + NBR // 2 : s * PAD + NBR // 2 + 1, :]

    own_x, own_inv = [], []
    zero3 = jnp.zeros((3, LANES), F32)
    for s in range(SLOTS):
        xs = [mid(x[v], s) for v in range(3)]
        inv = 1.0 / own_len[s]
        hi2, ns = inv * inv, mid(n2, s)
        own_x.append(jnp.concatenate(xs + [jnp.zeros((5, LANES), F32)], axis=0))
        own_inv.append(inv)
        scaled = jnp.concatenate([-2.0 * hi2 * v for v in xs] + [hi2, hi2 * ns, zero3], axis=0)
        plain = jnp.concatenate(
            [-2.0 * v for v in xs] + [jnp.ones((1, LANES), F32), ns, zero3], axis=0
        )
        for at, tile in ((s, scaled), (SLOTS + s, plain)):
            h, m, l = parts(tile, 3)
            big = jnp.concatenate([h, h, m, m, h, l, jnp.zeros((80, LANES), F32)], axis=0)
            ab[at] = jnp.transpose(big).astype(BF16)

    def make(step, k):
        a_at = jnp.where(step < SLOTS, step, step - SLOTS)
        b_at = jnp.where(step < 2 * SLOTS, step % SLOTS, step - SLOTS) * PAD
        t = bpart[pl.ds(pl.multiple_of((b_at + k) * 24, 8), 24), :]
        h, m, l = t[0:8], t[8:16], t[16:24]
        b = jnp.concatenate([h, m, h, m, l, h], axis=0).astype(BF16)
        sq[k * LANES : (k + 1) * LANES, :] = dot(ab[a_at][:, :48], b)

    def pair_pass(number, function, signs):
        def slot(s, _):
            after = jnp.minimum(number * SLOTS + s + 1, 3 * SLOTS - 1)
            total = jnp.zeros((16, LANES), F32)

            def work(k):
                for r in range(k * LANES, (k + 1) * LANES, CHUNK):
                    rows = slice(r, r + CHUNK)
                    hi_part[rows, :], lo_part[rows, :] = function(
                        jnp.maximum(sq[rows, :], TINY)
                    )

            def reduce(k):
                e = s * PAD + k
                rows = slice(k * LANES, (k + 1) * LANES)
                lhs = mtile[pl.ds(pl.multiple_of(e * 16, 16), 16), :]
                lhs = jnp.concatenate([lhs * f for f in signs], axis=1).astype(BF16)
                return dot(
                    lhs, jnp.concatenate([hi_part[rows, :], lo_part[rows, :]], axis=1), NT
                )

            for k in range(NBR):
                work(k)
                if k:
                    total = total + reduce(k - 1)
                    make(after, k - 1)
            total = total + reduce(NBR - 1)
            make(after, NBR - 1)
            acc[s] = total[0:8] + total[8:16]
            return 0

        lax.fori_loop(0, SLOTS, slot, 0)
        return [acc[s] for s in range(SLOTS)]

    def weight(q2):
        q = q2 * lax.rsqrt(q2)
        u = jnp.maximum(1.0 - q, 0.0)
        v = jnp.maximum(u - q, 0.0)
        return (u * u * u).astype(BF16), (v * v * v).astype(BF16)

    def slope(q2):
        inv_q = lax.rsqrt(q2)
        q = q2 * inv_q
        g = jnp.clip(inv_q, 1.0, 2.0) + jnp.maximum(-3.0 * q, jnp.minimum(q - 2.0, -1.0))
        high = g.astype(BF16)
        return high, (g - high.astype(F32)).astype(BF16)

    for k in range(NBR):
        make(0, k)
    sums = pair_pass(0, weight, (2.0, -1.0))
    rho_rows = []
    for s in range(SLOTS):
        rho_rows.append(NORM * sums[s][3:4] * own_inv[s] * own_inv[s] * own_inv[s])
    rho8 = jnp.concatenate(rho_rows + [jnp.ones((4, LANES), F32)], axis=0)
    rho[0] = rho8

    moved = jnp.sum(from_slot * exact_rows(rho8, pick_lane), axis=0, keepdims=True)
    fresh = jnp.where(is_new > 0.5, moved, state[6:7])
    full = jnp.where(sub8 == 6, fresh, state)
    ranked = jnp.concatenate(
        [
            jnp.where(rank < 0.5, full, 0.0),
            jnp.where(rank < 0.5, 0.0, full),
            jnp.zeros((112, LANES), F32),
        ],
        axis=0,
    )
    outb[...] = exact(to_dest, ranked, NT)

    rho_copies = [
        pltpu.make_async_remote_copy(
            src_ref=rho.at[0],
            dst_ref=rho.at[2 - side],
            send_sem=rho_send.at[side],
            recv_sem=rho_recv.at[side],
            device_id=target,
            device_id_type=MESH,
        )
        for side, target in enumerate(near)
    ]
    first_stage = []
    for k in range(1, n_gy):
        other = (gy + k) % n_gy
        first_stage.append(
            pltpu.make_async_remote_copy(
                src_ref=outb.at[pl.ds(pl.multiple_of(other * n_gx, n_gx), n_gx)],
                dst_ref=st1.at[pl.ds(pl.multiple_of(gy * n_gx, n_gx), n_gx)],
                send_sem=a_send.at[k],
                recv_sem=a_recv.at[k],
                device_id=(gx, other),
                device_id_type=MESH,
            )
        )
    for copy in rho_copies + first_stage:
        copy.start()
    mine = pl.ds(pl.multiple_of(gy * n_gx, n_gx), n_gx)
    st1[mine, :] = outb[mine, :]
    o_rho[...] = rho8

    for copy in late:
        copy.wait()
    gather(tiles2, ext2)
    inv_len = 1.0 / field(4)
    inv2 = inv_len * inv_len
    put_b(1, [x[0] * inv2, x[1] * inv2, x[2] * inv2, n2 * inv2, inv2])

    own_force = pair_pass(1, slope, (1.0, 1.0))

    for copy in first_stage:
        copy.wait()
    for a in range(n_gx):
        st2[a * n_gy : (a + 1) * n_gy, :] = st1[pl.ds(a, n_gy, stride=n_gx), :]
    second_stage = []
    for k in range(1, n_gx):
        other = (gx + k) % n_gx
        second_stage.append(
            pltpu.make_async_remote_copy(
                src_ref=st2.at[pl.ds(pl.multiple_of(other * n_gy, n_gy), n_gy)],
                dst_ref=st3.at[pl.ds(pl.multiple_of(gx * n_gy, n_gy), n_gy)],
                send_sem=b_send.at[k],
                recv_sem=b_recv.at[k],
                device_id=(other, gy),
                device_id_type=MESH,
            )
        )
    for copy in second_stage:
        copy.start()
    mine = pl.ds(pl.multiple_of(gx * n_gy, n_gy), n_gy)
    st3[mine, :] = st2[mine, :]

    for copy in rho_copies:
        copy.wait()

    candidates = jnp.concatenate([idt[0], idt[1], idt[2]], axis=0)
    wanted = jnp.full((1, LANES), -2, jnp.int32)
    lane1 = iota((1, LANES), 1)
    spread = jnp.concatenate(
        [nbr_mat[...], jnp.zeros((SLOTS, LANES - NBR), jnp.int32)], axis=1
    )
    for s in range(SLOTS):
        line = spread[s : s + 1]
        if s:
            line = pltpu.roll(line, s * PAD, 1)
        wanted = jnp.where((lane1 >= s * PAD) & (lane1 < s * PAD + NBR), line, wanted)
    match = (candidates == wanted.astype(F32)).astype(F32)
    match = jnp.transpose(jnp.concatenate([match, jnp.zeros((104, LANES), F32)], axis=0))
    news = jnp.concatenate([rho[0], rho[1], rho[2], jnp.zeros((104, LANES), F32)], axis=0)
    patch = exact(match.astype(BF16), news)
    hits = jnp.sum(match, axis=1, keepdims=True)
    dens = jnp.where(hits > 0.5, patch, field(6))
    inv5 = inv2 * inv2 * inv_len
    front = field(5) * jnp.exp(jnp.log(dens) * (-1.0 / 3.0)) * inv5
    factor = mass * front
    put_m([factor * x[0], factor * x[1], factor * x[2], factor])

    other_force = pair_pass(2, slope, (1.0, 1.0))

    for s in range(SLOTS):
        result = mid(front, s) * sums_of(own_force[s], own_x[s])
        result = (6.0 * NORM) * (result + sums_of(other_force[s], own_x[s]))
        o_acc[:, s, :] = jnp.where(s < cnt[0], result, 0.0)[0:3]

    for copy in second_stage:
        copy.wait()
    o_arr[...] = st3[...]


def finish(n_dev, act, cnt, base, den, rho, acc, rows, o_den, o_acc, o_arr):
    o_den[...] = den[...]
    for s in range(SLOTS):
        @pl.when(s < cnt[0])
        def _(s=s):
            o_den[pl.ds(act[s] - base[0], 1), :] = rho[s : s + 1, :]

    o_acc[...] = acc[...]
    turned = jnp.transpose(rows[...])
    halves = jnp.concatenate([turned[0:8], turned[8:16]], axis=1)
    width = 2 * n_dev
    source = iota((2 * LANES, width), 0)
    column = iota((2 * LANES, width), 1)
    spot = (source % LANES) * 2 + source // LANES
    spread = (spot == column).astype(F32).astype(BF16)
    o_arr[...] = exact_rows(halves, spread)[0:7]


def exact_rows(value, select):
    return sum(dot(part.astype(BF16), select) for part in parts(value, 3))


def sums_of(total, own_x):
    return own_x * total[3:4] - total


def local(
    n_gx,
    n_gy,
    positions,
    masses,
    smoothing,
    entropy,
    density,
    active_cells,
    active_count,
    neighbours,
    mig_source,
    mig_dest,
):
    smem = pl.BlockSpec(memory_space=pltpu.SMEM)
    vmem = pl.BlockSpec(memory_space=pltpu.VMEM)
    hbm = pl.BlockSpec(memory_space=pl.ANY)
    n_dev = n_gx * n_gy
    entries = SLOTS * PAD
    dma = pltpu.SemaphoreType.DMA
    rho, acc, rows = pl.pallas_call(
        functools.partial(kernel, n_gx, n_gy),
        out_shape=(
            jax.ShapeDtypeStruct((8, LANES), F32),
            jax.ShapeDtypeStruct((3, SLOTS, LANES), F32),
            jax.ShapeDtypeStruct((LANES, LANES), F32),
        ),
        in_specs=[smem] * 4 + [hbm] * 5 + [vmem] * 3,
        out_specs=(vmem, vmem, vmem),
        scratch_shapes=[
            pltpu.VMEM((8 * CELLS, LANES), F32),
            pltpu.VMEM((4 * EXT, LANES), F32),
            pltpu.VMEM((4 * EXT, LANES), F32),
            pltpu.VMEM((entries * 4, LANES), F32),
            pltpu.VMEM((entries * 4, LANES), F32),
            pltpu.VMEM((2 * entries * 24, LANES), F32),
            pltpu.VMEM((entries * 16, LANES), F32),
            pltpu.VMEM((2 * SLOTS, LANES, LANES), BF16),
            pltpu.VMEM((NBR * LANES, LANES), F32),
            pltpu.VMEM((NBR * LANES, LANES), BF16),
            pltpu.VMEM((NBR * LANES, LANES), BF16),
            pltpu.VMEM((SLOTS, 8, LANES), F32),
            pltpu.VMEM((3, 8, LANES), F32),
            pltpu.VMEM((3, 8, LANES), F32),
            pltpu.VMEM((LANES, LANES), F32),
            pltpu.VMEM((LANES, LANES), F32),
            pltpu.VMEM((LANES, LANES), F32),
            pltpu.VMEM((LANES, LANES), F32),
            dma((2, 7)),
            dma((2, 7)),
            dma((2, 7)),
            dma((2,)),
            dma((2,)),
            dma((2,)),
            dma((2,)),
            dma((n_gy,)),
            dma((n_gy,)),
            dma((n_gx,)),
            dma((n_gx,)),
        ],
        compiler_params=pltpu.CompilerParams(collective_id=0, has_side_effects=True),
    )(
        active_cells,
        active_count,
        neighbours,
        mig_source,
        positions,
        masses,
        smoothing,
        entropy,
        density,
        mig_source.reshape(1, ROWS),
        mig_dest.reshape(1, ROWS),
        neighbours,
    )
    base = (lax.axis_index(("gx", "gy")) * CELLS).astype(jnp.int32).reshape(1)
    return pl.pallas_call(
        functools.partial(finish, n_dev),
        out_shape=(
            jax.ShapeDtypeStruct((CELLS, LANES), F32),
            jax.ShapeDtypeStruct((3, SLOTS, LANES), F32),
            jax.ShapeDtypeStruct((7, 2 * n_dev), F32),
        ),
        in_specs=[smem] * 3 + [vmem] * 4,
        out_specs=(vmem, vmem, vmem),
    )(active_cells, active_count, base, density, rho, acc, rows)


def solution(mesh):
    both = ("gx", "gy")
    placed = (
        P(None, both, None),
        P(both, None),
        P(both, None),
        P(both, None),
        P(both, None),
        P(both),
        P(both),
        P(both, None),
        P(both),
        P(both, None),
    )
    return jax.shard_map(
        functools.partial(local, mesh.shape["gx"], mesh.shape["gy"]),
        mesh=mesh,
        in_specs=placed,
        out_specs=(P(both, None), P(None, both, None), P(None, both)),
        check_vma=False,
    )
```

```python
import functools
import math

import jax
import jax.numpy as jnp
from jax import lax
from jax.experimental import pallas as pl
from jax.experimental.pallas import tpu as pltpu
from jax.sharding import PartitionSpec as P

CELLS = 256
LANES = 128
RIM = 64
EXT = CELLS + 2 * RIM
NBR = 27
PAD = 32
SLOTS = 4
ROWS = 128
NORM = 8.0 / math.pi
TINY = 1e-12
CHUNK = 32

F32 = jnp.float32
BF16 = jnp.bfloat16
MESH = pl.DeviceIdType.MESH
NT = (((1,), (1,)), ((), ()))
NN = (((1,), (0,)), ((), ()))


def dot(a, b, dims=NN):
    return lax.dot_general(a, b, dims, preferred_element_type=F32)


def parts(value, count):
    out = []
    for _ in range(count - 1):
        head = value.astype(BF16).astype(F32)
        out.append(head)
        value = value - head
    out.append(value.astype(BF16).astype(F32))
    return out


def exact(select, value, dims=NN):
    return sum(dot(select, part.astype(BF16), dims) for part in parts(value, 3))


def iota(shape, dim):
    return lax.broadcasted_iota(jnp.int32, shape, dim)


def kernel(
    n_gx,
    n_gy,
    act_h,
    cnt_h,
    nbr_h,
    src_h,
    pos,
    mas,
    smo,
    ent,
    den,
    src_row_h,
    dst_row_h,
    o_rho,
    o_acc,
    o_arr,
    act,
    cnt,
    nbr,
    src,
    src_row,
    dst_row,
    nbr_mat,
    own,
    ext,
    ext2,
    tiles,
    tiles2,
    bpart,
    mtile,
    ab,
    sq,
    hi_part,
    lo_part,
    acc,
    idt,
    rho,
    outb,
    st1,
    st2,
    st3,
    small_sem,
    load_sem,
    rim_send,
    rim_recv,
    id_send,
    id_recv,
    rho_send,
    rho_recv,
    a_send,
    a_recv,
    b_send,
    b_recv,
):
    gx, gy = lax.axis_index("gx"), lax.axis_index("gy")
    n_dev = n_gx * n_gy
    me = gx * n_gy + gy
    prev, nxt = (me + n_dev - 1) % n_dev, (me + 1) % n_dev
    near = [(prev // n_gy, prev % n_gy), (nxt // n_gy, nxt % n_gy)]

    has = [me > 0, me < n_dev - 1]

    def start(side, copies):
        @pl.when(has[side])
        def _():
            for copy in copies:
                copy.start()

    def wait(side, copies):
        @pl.when(has[side])
        def _():
            for copy in copies:
                copy.wait_send()

        @pl.when(has[1 - side])
        def _():
            for copy in copies:
                copy.wait_recv()

    for at in (1, 2):
        idt[at] = jnp.full((8, LANES), -1.0, F32)
        rho[at] = jnp.ones((8, LANES), F32)

    barrier = pltpu.get_barrier_semaphore()
    for target in near:
        pl.semaphore_signal(barrier, inc=1, device_id=target, device_id_type=MESH)
    for k in range(1, n_gy):
        pl.semaphore_signal(
            barrier, inc=1, device_id=(gx, (gy + k) % n_gy), device_id_type=MESH
        )
    for k in range(1, n_gx):
        pl.semaphore_signal(
            barrier, inc=1, device_id=((gx + k) % n_gx, gy), device_id_type=MESH
        )

    fields = [pos.at[0], pos.at[1], pos.at[2], mas, smo, ent, den]

    def place_of(v, row, rows):
        if v < 4:
            return ext.at[pl.ds(v * EXT + row, rows)]
        return ext2.at[pl.ds((v - 4) * EXT + row, rows)]

    loads = [
        pltpu.make_async_copy(f, own.at[pl.ds(v * CELLS, CELLS)], load_sem.at[0, v])
        for v, f in enumerate(fields)
    ]
    fills = [
        pltpu.make_async_copy(f, place_of(v, RIM, CELLS), load_sem.at[1, v])
        for v, f in enumerate(fields)
    ]
    small = [
        pltpu.make_async_copy(a, b, small_sem.at[i])
        for i, (a, b) in enumerate(
            [
                (act_h, act),
                (cnt_h, cnt),
                (dst_row_h, dst_row),
                (src_row_h, src_row),
                (src_h, src),
                (nbr_h, nbr),
                (nbr_h, nbr_mat),
            ]
        )
    ]
    for copy in small + loads + fills:
        copy.start()
    pl.semaphore_wait(barrier, 2 + n_gy - 1 + n_gx - 1)
    def rim(side, v):
        first = 0 if side == 0 else CELLS - RIM
        land = RIM + CELLS if side == 0 else 0
        return pltpu.make_async_remote_copy(
            src_ref=fields[v].at[pl.ds(first, RIM)],
            dst_ref=place_of(v, land, RIM),
            send_sem=rim_send.at[side, v],
            recv_sem=rim_recv.at[side, v],
            device_id=near[side],
            device_id_type=MESH,
        )

    early = [[rim(side, v) for v in range(4)] for side in range(2)]
    late = [[rim(side, v) for v in range(4, 7)] for side in range(2)]
    for side, target in enumerate(near):
        late[side].append(
            pltpu.make_async_remote_copy(
                src_ref=idt.at[0],
                dst_ref=idt.at[2 - side],
                send_sem=id_send.at[side],
                recv_sem=id_recv.at[side],
                device_id=target,
                device_id_type=MESH,
            )
        )
    for side in range(2):
        start(side, early[side])
    for copy in small:
        copy.wait()

    base = me * CELLS
    sub8 = iota((8, LANES), 0)
    ids = jnp.full((8, LANES), -1, jnp.int32)
    for s in range(SLOTS):
        ids = jnp.where((sub8 == s) & (s < cnt[0]), act[s], ids)
    idt[0] = ids.astype(F32)
    ext2[pl.ds(3 * EXT, EXT), :] = jnp.zeros((EXT, LANES), F32)
    own[pl.ds(7 * CELLS, CELLS), :] = jnp.zeros((CELLS, LANES), F32)

    dest = dst_row[...]
    place = (dest % n_gy) * n_gx + dest // n_gy
    to_dest = (iota((LANES, ROWS), 0) == place).astype(F32)
    earlier = (iota((ROWS, ROWS), 0) < iota((ROWS, ROWS), 1)).astype(F32)
    before = dot(to_dest.astype(BF16), earlier.astype(BF16))
    rank = jnp.sum(to_dest * before, axis=0, keepdims=True)
    to_dest = to_dest.astype(BF16)
    src_cell = src_row[...] // LANES
    src_lane = src_row[...] % LANES
    pick_lane = (iota((LANES, ROWS), 0) == src_lane).astype(F32).astype(BF16)
    from_slot = ((src_cell + base).astype(F32) == idt[0]).astype(F32)
    is_new = jnp.sum(from_slot, axis=0, keepdims=True)

    for copy in loads:
        copy.wait()

    lane8 = iota((8, LANES), 1)

    def mig_row(r, state):
        where_from = src[r]
        tile = own[pl.ds(where_from // LANES, 8, stride=CELLS), :]
        value = jnp.sum(
            jnp.where(lane8 == where_from % LANES, tile, 0.0), axis=1, keepdims=True
        )
        return jnp.where(lane8 == r, value, state)

    state = lax.fori_loop(0, ROWS, mig_row, jnp.zeros((8, LANES), F32), unroll=8)
    own_len = []
    for s in range(SLOTS):
        row = jnp.clip(act[s] - base, 0, CELLS - 1)
        own_len.append(own[pl.ds(row + 4 * CELLS, 1), :])
    for s in range(SLOTS):
        for t in (tiles, tiles2):
            t[(s * PAD + NBR) * 4 : (s + 1) * PAD * 4, :] = jnp.ones(
                ((PAD - NBR) * 4, LANES), F32
            )
    bpart[...] = jnp.zeros_like(bpart)
    mtile[...] = jnp.zeros_like(mtile)

    for copy in fills:
        copy.wait()
    for side in range(2):
        wait(side, early[side])
        start(side, late[side])

    def gather(into, out_of):
        for s in range(SLOTS):
            def fetch(k, _, s=s):
                cell = jnp.clip(nbr[s, k] - (base - RIM), 0, EXT - 1)
                into[pl.ds((s * PAD + k) * 4, 4), :] = out_of[pl.ds(cell, 4, stride=EXT), :]
                return 0

            lax.fori_loop(0, NBR, fetch, 0, unroll=9)

    entries = SLOTS * PAD
    gather(tiles, ext)
    k_of = iota((entries, LANES), 0) % PAD
    offset = [k_of // 9 - 1, (k_of // 3) % 3 - 1, k_of % 3 - 1]

    def field(v):
        ref = tiles if v < 4 else tiles2
        return ref[pl.ds(v % 4, entries, stride=4), :]

    x = [field(v) - 0.5 + offset[v].astype(F32) for v in range(3)]
    mass = field(3)
    n2 = x[0] * x[0] + x[1] * x[1] + x[2] * x[2]

    def put_b(at, values):
        for c, value in enumerate(values):
            for p, part in enumerate(parts(value, 3)):
                bpart[pl.ds(at * entries * 24 + p * 8 + c, entries, stride=24), :] = part

    def put_m(values):
        for c, value in enumerate(values):
            for p, part in enumerate(parts(value, 2)):
                mtile[pl.ds(p * 8 + c, entries, stride=16), :] = part

    one = jnp.ones((entries, LANES), F32)
    put_b(0, [x[0], x[1], x[2], n2, one])
    put_m([mass * x[0], mass * x[1], mass * x[2], mass])

    def mid(value, s):
        return value[s * PAD + NBR // 2 : s * PAD + NBR // 2 + 1, :]

    own_x, own_inv = [], []
    zero3 = jnp.zeros((3, LANES), F32)
    for s in range(SLOTS):
        xs = [mid(x[v], s) for v in range(3)]
        inv = 1.0 / own_len[s]
        hi2, ns = inv * inv, mid(n2, s)
        own_x.append(jnp.concatenate(xs + [jnp.zeros((5, LANES), F32)], axis=0))
        own_inv.append(inv)
        scaled = jnp.concatenate([-2.0 * hi2 * v for v in xs] + [hi2, hi2 * ns, zero3], axis=0)
        plain = jnp.concatenate(
            [-2.0 * v for v in xs] + [jnp.ones((1, LANES), F32), ns, zero3], axis=0
        )
        for at, tile in ((s, scaled), (SLOTS + s, plain)):
            h, m, l = parts(tile, 3)
            big = jnp.concatenate([h, h, m, m, h, l, jnp.zeros((80, LANES), F32)], axis=0)
            ab[at] = jnp.transpose(big).astype(BF16)

    def make(step, k):
        a_at = jnp.where(step < SLOTS, step, step - SLOTS)
        b_at = jnp.where(step < 2 * SLOTS, step % SLOTS, step - SLOTS) * PAD
        t = bpart[pl.ds(pl.multiple_of((b_at + k) * 24, 8), 24), :]
        h, m, l = t[0:8], t[8:16], t[16:24]
        b = jnp.concatenate([h, m, h, m, l, h], axis=0).astype(BF16)
        sq[k * LANES : (k + 1) * LANES, :] = dot(ab[a_at][:, :48], b)

    def pair_pass(number, function, signs, first=0, last=SLOTS):
        def slot(s, _):
            after = jnp.minimum(number * SLOTS + s + 1, 3 * SLOTS - 1)
            total = jnp.zeros((16, LANES), F32)

            def work(k):
                for r in range(k * LANES, (k + 1) * LANES, CHUNK):
                    rows = slice(r, r + CHUNK)
                    hi_part[rows, :], lo_part[rows, :] = function(
                        jnp.maximum(sq[rows, :], TINY)
                    )

            def reduce(k):
                e = s * PAD + k
                rows = slice(k * LANES, (k + 1) * LANES)
                lhs = mtile[pl.ds(pl.multiple_of(e * 16, 16), 16), :]
                lhs = jnp.concatenate([lhs * f for f in signs], axis=1).astype(BF16)
                return dot(
                    lhs, jnp.concatenate([hi_part[rows, :], lo_part[rows, :]], axis=1), NT
                )

            for k in range(NBR):
                work(k)
                if k:
                    total = total + reduce(k - 1)
                    make(after, k - 1)
            total = total + reduce(NBR - 1)
            make(after, NBR - 1)
            acc[s] = total[0:8] + total[8:16]
            return 0

        lax.fori_loop(first, last, slot, 0)
        return [acc[s] for s in range(SLOTS)]

    def weight(q2):
        q = q2 * lax.rsqrt(q2)
        u = jnp.maximum(1.0 - q, 0.0)
        v = jnp.maximum(u - q, 0.0)
        return (u * u * u).astype(BF16), (v * v * v).astype(BF16)

    def slope(q2):
        inv_q = lax.rsqrt(q2)
        q = q2 * inv_q
        g = jnp.clip(inv_q, 1.0, 2.0) + jnp.maximum(-3.0 * q, jnp.minimum(q - 2.0, -1.0))
        high = g.astype(BF16)
        return high, (g - high.astype(F32)).astype(BF16)

    for k in range(NBR):
        make(0, k)
    sums = pair_pass(0, weight, (2.0, -1.0))
    rho_rows = []
    for s in range(SLOTS):
        rho_rows.append(NORM * sums[s][3:4] * own_inv[s] * own_inv[s] * own_inv[s])
    rho8 = jnp.concatenate(rho_rows + [jnp.ones((4, LANES), F32)], axis=0)
    rho[0] = rho8

    moved = jnp.sum(from_slot * exact_rows(rho8, pick_lane), axis=0, keepdims=True)
    fresh = jnp.where(is_new > 0.5, moved, state[6:7])
    full = jnp.where(sub8 == 6, fresh, state)
    ranked = jnp.concatenate(
        [
            jnp.where(rank < 0.5, full, 0.0),
            jnp.where(rank < 0.5, 0.0, full),
            jnp.zeros((112, LANES), F32),
        ],
        axis=0,
    )
    outb[...] = exact(to_dest, ranked, NT)

    rho_copies = [
        pltpu.make_async_remote_copy(
            src_ref=rho.at[0],
            dst_ref=rho.at[2 - side],
            send_sem=rho_send.at[side],
            recv_sem=rho_recv.at[side],
            device_id=target,
            device_id_type=MESH,
        )
        for side, target in enumerate(near)
    ]
    first_stage = []
    for k in range(1, n_gy):
        other = (gy + k) % n_gy
        first_stage.append(
            pltpu.make_async_remote_copy(
                src_ref=outb.at[pl.ds(pl.multiple_of(other * n_gx, n_gx), n_gx)],
                dst_ref=st1.at[pl.ds(pl.multiple_of(gy * n_gx, n_gx), n_gx)],
                send_sem=a_send.at[k],
                recv_sem=a_recv.at[k],
                device_id=(gx, other),
                device_id_type=MESH,
            )
        )
    for side in range(2):
        start(side, rho_copies[side : side + 1])
    for copy in first_stage:
        copy.start()
    mine = pl.ds(pl.multiple_of(gy * n_gx, n_gx), n_gx)
    st1[mine, :] = outb[mine, :]
    o_rho[...] = rho8

    for side in range(2):
        wait(side, late[side])
    gather(tiles2, ext2)
    inv_len = 1.0 / field(4)
    inv2 = inv_len * inv_len
    put_b(1, [x[0] * inv2, x[1] * inv2, x[2] * inv2, n2 * inv2, inv2])

    pair_pass(1, slope, (1.0, 1.0), 0, SLOTS - 1)

    for copy in first_stage:
        copy.wait()
    for a in range(n_gx):
        st2[a * n_gy : (a + 1) * n_gy, :] = st1[pl.ds(a, n_gy, stride=n_gx), :]
    second_stage = []
    for k in range(1, n_gx):
        other = (gx + k) % n_gx
        second_stage.append(
            pltpu.make_async_remote_copy(
                src_ref=st2.at[pl.ds(pl.multiple_of(other * n_gy, n_gy), n_gy)],
                dst_ref=st3.at[pl.ds(pl.multiple_of(gx * n_gy, n_gy), n_gy)],
                send_sem=b_send.at[k],
                recv_sem=b_recv.at[k],
                device_id=(other, gy),
                device_id_type=MESH,
            )
        )
    for copy in second_stage:
        copy.start()
    mine = pl.ds(pl.multiple_of(gx * n_gy, n_gy), n_gy)
    st3[mine, :] = st2[mine, :]
    own_force = pair_pass(1, slope, (1.0, 1.0), SLOTS - 1, SLOTS)

    for side in range(2):
        wait(side, rho_copies[side : side + 1])

    candidates = jnp.concatenate([idt[0], idt[1], idt[2]], axis=0)
    wanted = jnp.full((1, LANES), -2, jnp.int32)
    lane1 = iota((1, LANES), 1)
    spread = jnp.concatenate(
        [nbr_mat[...], jnp.zeros((SLOTS, LANES - NBR), jnp.int32)], axis=1
    )
    for s in range(SLOTS):
        line = spread[s : s + 1]
        if s:
            line = pltpu.roll(line, s * PAD, 1)
        wanted = jnp.where((lane1 >= s * PAD) & (lane1 < s * PAD + NBR), line, wanted)
    match = (candidates == wanted.astype(F32)).astype(F32)
    match = jnp.transpose(jnp.concatenate([match, jnp.zeros((104, LANES), F32)], axis=0))
    news = jnp.concatenate([rho[0], rho[1], rho[2], jnp.zeros((104, LANES), F32)], axis=0)
    patch = exact(match.astype(BF16), news)
    hits = jnp.sum(match, axis=1, keepdims=True)
    dens = jnp.where(hits > 0.5, patch, field(6))
    inv5 = inv2 * inv2 * inv_len
    front = field(5) * jnp.exp(jnp.log(dens) * (-1.0 / 3.0)) * inv5
    factor = mass * front
    put_m([factor * x[0], factor * x[1], factor * x[2], factor])

    other_force = pair_pass(2, slope, (1.0, 1.0))

    for s in range(SLOTS):
        result = mid(front, s) * sums_of(own_force[s], own_x[s])
        result = (6.0 * NORM) * (result + sums_of(other_force[s], own_x[s]))
        o_acc[:, s, :] = jnp.where(s < cnt[0], result, 0.0)[0:3]

    for copy in second_stage:
        copy.wait()
    o_arr[...] = st3[...]


def finish(n_gx, n_gy, act, cnt, den, rho, acc, rows, o_den, o_acc, o_arr):
    base = (lax.axis_index("gx") * n_gy + lax.axis_index("gy")) * CELLS
    o_den[...] = den[...]
    for s in range(SLOTS):
        @pl.when(s < cnt[0])
        def _(s=s):
            o_den[pl.ds(jnp.clip(act[s] - base, 0, CELLS - 1), 1), :] = rho[s : s + 1, :]

    o_acc[...] = acc[...]
    turned = jnp.transpose(rows[...])
    halves = jnp.concatenate([turned[0:8], turned[8:16]], axis=1)
    width = 2 * n_gx * n_gy
    source = iota((2 * LANES, width), 0)
    column = iota((2 * LANES, width), 1)
    spot = (source % LANES) * 2 + source // LANES
    spread = (spot == column).astype(F32).astype(BF16)
    o_arr[...] = exact_rows(halves, spread)[0:7]


def exact_rows(value, select):
    return sum(dot(part.astype(BF16), select) for part in parts(value, 3))


def sums_of(total, own_x):
    return own_x * total[3:4] - total


def local(
    n_gx,
    n_gy,
    positions,
    masses,
    smoothing,
    entropy,
    density,
    active_cells,
    active_count,
    neighbours,
    mig_source,
    mig_dest,
):
    smem = pl.BlockSpec(memory_space=pltpu.SMEM)
    vmem = pl.BlockSpec(memory_space=pltpu.VMEM)
    hbm = pl.BlockSpec(memory_space=pl.ANY)
    n_dev = n_gx * n_gy
    entries = SLOTS * PAD
    dma = pltpu.SemaphoreType.DMA
    rho, acc, rows = pl.pallas_call(
        functools.partial(kernel, n_gx, n_gy),
        out_shape=(
            jax.ShapeDtypeStruct((8, LANES), F32),
            jax.ShapeDtypeStruct((3, SLOTS, LANES), F32),
            jax.ShapeDtypeStruct((LANES, LANES), F32),
        ),
        in_specs=[hbm] * 11,
        out_specs=(vmem, vmem, vmem),
        scratch_shapes=[
            pltpu.SMEM((SLOTS,), jnp.int32),
            pltpu.SMEM((1,), jnp.int32),
            pltpu.SMEM((SLOTS, NBR), jnp.int32),
            pltpu.SMEM((ROWS,), jnp.int32),
            pltpu.VMEM((1, ROWS), jnp.int32),
            pltpu.VMEM((1, ROWS), jnp.int32),
            pltpu.VMEM((SLOTS, NBR), jnp.int32),
            pltpu.VMEM((8 * CELLS, LANES), F32),
            pltpu.VMEM((4 * EXT, LANES), F32),
            pltpu.VMEM((4 * EXT, LANES), F32),
            pltpu.VMEM((entries * 4, LANES), F32),
            pltpu.VMEM((entries * 4, LANES), F32),
            pltpu.VMEM((2 * entries * 24, LANES), F32),
            pltpu.VMEM((entries * 16, LANES), F32),
            pltpu.VMEM((2 * SLOTS, LANES, LANES), BF16),
            pltpu.VMEM((NBR * LANES, LANES), F32),
            pltpu.VMEM((NBR * LANES, LANES), BF16),
            pltpu.VMEM((NBR * LANES, LANES), BF16),
            pltpu.VMEM((SLOTS, 8, LANES), F32),
            pltpu.VMEM((3, 8, LANES), F32),
            pltpu.VMEM((3, 8, LANES), F32),
            pltpu.VMEM((LANES, LANES), F32),
            pltpu.VMEM((LANES, LANES), F32),
            pltpu.VMEM((LANES, LANES), F32),
            pltpu.VMEM((LANES, LANES), F32),
            dma((7,)),
            dma((2, 7)),
            dma((2, 7)),
            dma((2, 7)),
            dma((2,)),
            dma((2,)),
            dma((2,)),
            dma((2,)),
            dma((n_gy,)),
            dma((n_gy,)),
            dma((n_gx,)),
            dma((n_gx,)),
        ],
        compiler_params=pltpu.CompilerParams(collective_id=0, has_side_effects=True),
    )(
        active_cells,
        active_count,
        neighbours,
        mig_source,
        positions,
        masses,
        smoothing,
        entropy,
        density,
        mig_source.reshape(1, ROWS),
        mig_dest.reshape(1, ROWS),
    )
    return pl.pallas_call(
        functools.partial(finish, n_gx, n_gy),
        out_shape=(
            jax.ShapeDtypeStruct((CELLS, LANES), F32),
            jax.ShapeDtypeStruct((3, SLOTS, LANES), F32),
            jax.ShapeDtypeStruct((7, 2 * n_dev), F32),
        ),
        in_specs=[smem] * 2 + [vmem] * 4,
        out_specs=(vmem, vmem, vmem),
    )(active_cells, active_count, density, rho, acc, rows)


def solution(mesh):
    both = ("gx", "gy")
    placed = (
        P(None, both, None),
        P(both, None),
        P(both, None),
        P(both, None),
        P(both, None),
        P(both),
        P(both),
        P(both, None),
        P(both),
        P(both, None),
    )
    return jax.shard_map(
        functools.partial(local, mesh.shape["gx"], mesh.shape["gy"]),
        mesh=mesh,
        in_specs=placed,
        out_specs=(P(both, None), P(None, both, None), P(None, both)),
        check_vma=False,
    )
```

```python
import functools
import math

import jax
import jax.numpy as jnp
from jax import lax
from jax.experimental import pallas as pl
from jax.experimental.pallas import tpu as pltpu
from jax.sharding import PartitionSpec as P

CELLS = 256
LANES = 128
RIM = 64
EXT = CELLS + 2 * RIM
NBR = 27
PAD = 32
SLOTS = 4
ROWS = 128
NORM = 8.0 / math.pi
TINY = 1e-12
CHUNK = 32

F32 = jnp.float32
BF16 = jnp.bfloat16
MESH = pl.DeviceIdType.MESH
NT = (((1,), (1,)), ((), ()))
NN = (((1,), (0,)), ((), ()))


def dot(a, b, dims=NN):
    return lax.dot_general(a, b, dims, preferred_element_type=F32)


def parts(value, count):
    out = []
    for _ in range(count - 1):
        head = value.astype(BF16).astype(F32)
        out.append(head)
        value = value - head
    out.append(value.astype(BF16).astype(F32))
    return out


def exact(select, value, dims=NN):
    return sum(dot(select, part.astype(BF16), dims) for part in parts(value, 3))


def iota(shape, dim):
    return lax.broadcasted_iota(jnp.int32, shape, dim)


def kernel(
    n_gx,
    n_gy,
    act_h,
    cnt_h,
    nbr_h,
    src_h,
    pos,
    mas,
    smo,
    ent,
    den,
    src_row_h,
    dst_row_h,
    o_rho,
    o_acc,
    o_arr,
    act,
    cnt,
    nbr,
    src,
    src_row,
    dst_row,
    nbr_mat,
    own,
    ext,
    ext2,
    tiles,
    tiles2,
    bpart,
    mtile,
    ab,
    sq,
    hi_part,
    lo_part,
    acc,
    idt,
    rho,
    outb,
    st1,
    st2,
    st3,
    small_sem,
    load_sem,
    rim_send,
    rim_recv,
    id_send,
    id_recv,
    rho_send,
    rho_recv,
    a_send,
    a_recv,
    b_send,
    b_recv,
):
    gx, gy = lax.axis_index("gx"), lax.axis_index("gy")
    n_dev = n_gx * n_gy
    me = gx * n_gy + gy
    prev, nxt = (me + n_dev - 1) % n_dev, (me + 1) % n_dev
    near = [(prev // n_gy, prev % n_gy), (nxt // n_gy, nxt % n_gy)]

    has = [me > 0, me < n_dev - 1]

    def start(side, copies):
        @pl.when(has[side])
        def _():
            for copy in copies:
                copy.start()

    def wait(side, copies):
        @pl.when(has[side])
        def _():
            for copy in copies:
                copy.wait_send()

        @pl.when(has[1 - side])
        def _():
            for copy in copies:
                copy.wait_recv()

    for at in (1, 2):
        idt[at] = jnp.full((8, LANES), -1.0, F32)
        rho[at] = jnp.ones((8, LANES), F32)

    barrier = pltpu.get_barrier_semaphore()
    for target in near:
        pl.semaphore_signal(barrier, inc=1, device_id=target, device_id_type=MESH)
    for k in range(1, n_gy):
        pl.semaphore_signal(
            barrier, inc=1, device_id=(gx, (gy + k) % n_gy), device_id_type=MESH
        )
    for k in range(1, n_gx):
        pl.semaphore_signal(
            barrier, inc=1, device_id=((gx + k) % n_gx, gy), device_id_type=MESH
        )

    fields = [pos.at[0], pos.at[1], pos.at[2], mas, smo, ent, den]

    def place_of(v, row, rows):
        if v < 4:
            return ext.at[pl.ds(v * EXT + row, rows)]
        return ext2.at[pl.ds((v - 4) * EXT + row, rows)]

    loads = [
        pltpu.make_async_copy(f, own.at[pl.ds(v * CELLS, CELLS)], load_sem.at[0, v])
        for v, f in enumerate(fields)
    ]
    fills = [
        pltpu.make_async_copy(f, place_of(v, RIM, CELLS), load_sem.at[1, v])
        for v, f in enumerate(fields)
    ]
    small = [
        pltpu.make_async_copy(a, b, small_sem.at[i])
        for i, (a, b) in enumerate(
            [
                (act_h, act),
                (cnt_h, cnt),
                (dst_row_h, dst_row),
                (src_row_h, src_row),
                (src_h, src),
                (nbr_h, nbr),
                (nbr_h, nbr_mat),
            ]
        )
    ]
    for copy in small + loads + fills:
        copy.start()
    pl.semaphore_wait(barrier, 2 + n_gy - 1 + n_gx - 1)
    def rim(side, v):
        first = 0 if side == 0 else CELLS - RIM
        land = RIM + CELLS if side == 0 else 0
        return pltpu.make_async_remote_copy(
            src_ref=fields[v].at[pl.ds(first, RIM)],
            dst_ref=place_of(v, land, RIM),
            send_sem=rim_send.at[side, v],
            recv_sem=rim_recv.at[side, v],
            device_id=near[side],
            device_id_type=MESH,
        )

    early = [[rim(side, v) for v in range(4)] for side in range(2)]
    late = [[rim(side, v) for v in range(4, 7)] for side in range(2)]
    for side, target in enumerate(near):
        late[side].append(
            pltpu.make_async_remote_copy(
                src_ref=idt.at[0],
                dst_ref=idt.at[2 - side],
                send_sem=id_send.at[side],
                recv_sem=id_recv.at[side],
                device_id=target,
                device_id_type=MESH,
            )
        )
    for side in range(2):
        start(side, early[side])
    for copy in small:
        copy.wait()

    base = me * CELLS
    sub8 = iota((8, LANES), 0)
    ids = jnp.full((8, LANES), -1, jnp.int32)
    for s in range(SLOTS):
        ids = jnp.where((sub8 == s) & (s < cnt[0]), act[s], ids)
    idt[0] = ids.astype(F32)
    ext2[pl.ds(3 * EXT, EXT), :] = jnp.zeros((EXT, LANES), F32)
    own[pl.ds(7 * CELLS, CELLS), :] = jnp.zeros((CELLS, LANES), F32)

    dest = dst_row[...]
    place = (dest % n_gy) * n_gx + dest // n_gy
    to_dest = (iota((LANES, ROWS), 0) == place).astype(F32)
    earlier = (iota((ROWS, ROWS), 0) < iota((ROWS, ROWS), 1)).astype(F32)
    before = dot(to_dest.astype(BF16), earlier.astype(BF16))
    rank = jnp.sum(to_dest * before, axis=0, keepdims=True)
    to_dest = to_dest.astype(BF16)
    src_cell = src_row[...] // LANES
    src_lane = src_row[...] % LANES
    pick_lane = (iota((LANES, ROWS), 0) == src_lane).astype(F32).astype(BF16)
    from_slot = ((src_cell + base).astype(F32) == idt[0]).astype(F32)
    is_new = jnp.sum(from_slot, axis=0, keepdims=True)

    for copy in loads:
        copy.wait()

    lane8 = iota((8, LANES), 1)

    def mig_row(r, state):
        where_from = src[r]
        tile = own[pl.ds(where_from // LANES, 8, stride=CELLS), :]
        value = jnp.sum(
            jnp.where(lane8 == where_from % LANES, tile, 0.0), axis=1, keepdims=True
        )
        return jnp.where(lane8 == r, value, state)

    state = lax.fori_loop(0, ROWS, mig_row, jnp.zeros((8, LANES), F32), unroll=8)
    own_len = []
    for s in range(SLOTS):
        row = jnp.clip(act[s] - base, 0, CELLS - 1)
        own_len.append(own[pl.ds(row + 4 * CELLS, 1), :])
    for s in range(SLOTS):
        for t in (tiles, tiles2):
            t[(s * PAD + NBR) * 4 : (s + 1) * PAD * 4, :] = jnp.ones(
                ((PAD - NBR) * 4, LANES), F32
            )
    bpart[...] = jnp.zeros_like(bpart)
    mtile[...] = jnp.zeros_like(mtile)

    for copy in fills:
        copy.wait()
    for side in range(2):
        wait(side, early[side])
        start(side, late[side])

    def gather(into, out_of):
        for s in range(SLOTS):
            def fetch(k, _, s=s):
                cell = jnp.clip(nbr[s, k] - (base - RIM), 0, EXT - 1)
                into[pl.ds((s * PAD + k) * 4, 4), :] = out_of[pl.ds(cell, 4, stride=EXT), :]
                return 0

            lax.fori_loop(0, NBR, fetch, 0, unroll=9)

    entries = SLOTS * PAD
    gather(tiles, ext)
    k_of = iota((entries, LANES), 0) % PAD
    offset = [k_of // 9 - 1, (k_of // 3) % 3 - 1, k_of % 3 - 1]

    def field(v):
        ref = tiles if v < 4 else tiles2
        return ref[pl.ds(v % 4, entries, stride=4), :]

    x = [field(v) - 0.5 + offset[v].astype(F32) for v in range(3)]
    mass = field(3)
    n2 = x[0] * x[0] + x[1] * x[1] + x[2] * x[2]

    def put_b(at, values):
        for c, value in enumerate(values):
            for p, part in enumerate(parts(value, 3)):
                bpart[pl.ds(at * entries * 24 + p * 8 + c, entries, stride=24), :] = part

    def put_m(values):
        for c, value in enumerate(values):
            for p, part in enumerate(parts(value, 2)):
                mtile[pl.ds(p * 8 + c, entries, stride=16), :] = part

    one = jnp.ones((entries, LANES), F32)
    put_b(0, [x[0], x[1], x[2], n2, one])
    put_m([mass * x[0], mass * x[1], mass * x[2], mass])

    def mid(value, s):
        return value[s * PAD + NBR // 2 : s * PAD + NBR // 2 + 1, :]

    own_x, own_inv = [], []
    zero3 = jnp.zeros((3, LANES), F32)
    for s in range(SLOTS):
        xs = [mid(x[v], s) for v in range(3)]
        inv = 1.0 / own_len[s]
        hi2, ns = inv * inv, mid(n2, s)
        own_x.append(jnp.concatenate(xs + [jnp.zeros((5, LANES), F32)], axis=0))
        own_inv.append(inv)
        scaled = jnp.concatenate([-2.0 * hi2 * v for v in xs] + [hi2, hi2 * ns, zero3], axis=0)
        plain = jnp.concatenate(
            [-2.0 * v for v in xs] + [jnp.ones((1, LANES), F32), ns, zero3], axis=0
        )
        for at, tile in ((s, scaled), (SLOTS + s, plain)):
            h, m, l = parts(tile, 3)
            big = jnp.concatenate([h, h, m, m, h, l, jnp.zeros((80, LANES), F32)], axis=0)
            ab[at] = jnp.transpose(big).astype(BF16)

    def make(step, k):
        a_at = jnp.where(step < SLOTS, step, step - SLOTS)
        b_at = jnp.where(step < 2 * SLOTS, step % SLOTS, step - SLOTS) * PAD
        t = bpart[pl.ds(pl.multiple_of((b_at + k) * 24, 8), 24), :]
        h, m, l = t[0:8], t[8:16], t[16:24]
        b = jnp.concatenate([h, m, h, m, l, h], axis=0).astype(BF16)
        sq[k * LANES : (k + 1) * LANES, :] = dot(ab[a_at][:, :48], b)

    def pair_pass(number, function, signs, first=0, last=SLOTS):
        def slot(s, _):
            after = jnp.minimum(number * SLOTS + s + 1, 3 * SLOTS - 1)
            total = jnp.zeros((16, LANES), F32)

            def work(k):
                for r in range(k * LANES, (k + 1) * LANES, CHUNK):
                    rows = slice(r, r + CHUNK)
                    hi_part[rows, :], lo_part[rows, :] = function(
                        jnp.maximum(sq[rows, :], TINY)
                    )

            def reduce(k):
                e = s * PAD + k
                rows = slice(k * LANES, (k + 1) * LANES)
                lhs = mtile[pl.ds(pl.multiple_of(e * 16, 16), 16), :]
                lhs = jnp.concatenate([lhs * f for f in signs], axis=1).astype(BF16)
                return dot(
                    lhs, jnp.concatenate([hi_part[rows, :], lo_part[rows, :]], axis=1), NT
                )

            for k in range(NBR):
                work(k)
                if k:
                    total = total + reduce(k - 1)
                    make(after, k - 1)
            total = total + reduce(NBR - 1)
            make(after, NBR - 1)
            acc[s] = total[0:8] + total[8:16]
            return 0

        lax.fori_loop(first, last, slot, 0)
        return [acc[s] for s in range(SLOTS)]

    def weight(q2):
        q = q2 * lax.rsqrt(q2)
        u = jnp.maximum(1.0 - q, 0.0)
        v = jnp.maximum(u - q, 0.0)
        return (u * u * u).astype(BF16), (v * v * v).astype(BF16)

    def slope(q2):
        inv_q = lax.rsqrt(q2)
        q = q2 * inv_q
        g = jnp.clip(inv_q, 1.0, 2.0) + jnp.maximum(-3.0 * q, jnp.minimum(q - 2.0, -1.0))
        high = g.astype(BF16)
        return high, (g - high.astype(F32)).astype(BF16)

    for k in range(NBR):
        make(0, k)
    sums = pair_pass(0, weight, (2.0, -1.0))
    rho_rows = []
    for s in range(SLOTS):
        rho_rows.append(NORM * sums[s][3:4] * own_inv[s] * own_inv[s] * own_inv[s])
    rho8 = jnp.concatenate(rho_rows + [jnp.ones((4, LANES), F32)], axis=0)
    rho[0] = rho8

    moved = jnp.sum(from_slot * exact_rows(rho8, pick_lane), axis=0, keepdims=True)
    fresh = jnp.where(is_new > 0.5, moved, state[6:7])
    full = jnp.where(sub8 == 6, fresh, state)
    ranked = jnp.concatenate(
        [
            jnp.where(rank < 0.5, full, 0.0),
            jnp.where(rank < 0.5, 0.0, full),
            jnp.zeros((112, LANES), F32),
        ],
        axis=0,
    )
    outb[...] = exact(to_dest, ranked, NT)

    rho_copies = [
        pltpu.make_async_remote_copy(
            src_ref=rho.at[0],
            dst_ref=rho.at[2 - side],
            send_sem=rho_send.at[side],
            recv_sem=rho_recv.at[side],
            device_id=target,
            device_id_type=MESH,
        )
        for side, target in enumerate(near)
    ]
    first_stage = []
    for k in range(1, n_gy):
        other = (gy + k) % n_gy
        first_stage.append(
            pltpu.make_async_remote_copy(
                src_ref=outb.at[pl.ds(pl.multiple_of(other * n_gx, n_gx), n_gx)],
                dst_ref=st1.at[pl.ds(pl.multiple_of(gy * n_gx, n_gx), n_gx)],
                send_sem=a_send.at[k],
                recv_sem=a_recv.at[k],
                device_id=(gx, other),
                device_id_type=MESH,
            )
        )
    for side in range(2):
        start(side, rho_copies[side : side + 1])
    for copy in first_stage:
        copy.start()
    mine = pl.ds(pl.multiple_of(gy * n_gx, n_gx), n_gx)
    st1[mine, :] = outb[mine, :]
    o_rho[0:8, :] = rho8
    o_rho[8:16, :] = idt[0]

    for side in range(2):
        wait(side, late[side])
    gather(tiles2, ext2)
    inv_len = 1.0 / field(4)
    inv2 = inv_len * inv_len
    put_b(1, [x[0] * inv2, x[1] * inv2, x[2] * inv2, n2 * inv2, inv2])

    pair_pass(1, slope, (1.0, 1.0), 0, SLOTS - 1)

    for copy in first_stage:
        copy.wait()
    for a in range(n_gx):
        st2[a * n_gy : (a + 1) * n_gy, :] = st1[pl.ds(a, n_gy, stride=n_gx), :]
    second_stage = []
    for k in range(1, n_gx):
        other = (gx + k) % n_gx
        second_stage.append(
            pltpu.make_async_remote_copy(
                src_ref=st2.at[pl.ds(pl.multiple_of(other * n_gy, n_gy), n_gy)],
                dst_ref=st3.at[pl.ds(pl.multiple_of(gx * n_gy, n_gy), n_gy)],
                send_sem=b_send.at[k],
                recv_sem=b_recv.at[k],
                device_id=(other, gy),
                device_id_type=MESH,
            )
        )
    for copy in second_stage:
        copy.start()
    mine = pl.ds(pl.multiple_of(gx * n_gy, n_gy), n_gy)
    st3[mine, :] = st2[mine, :]
    own_force = pair_pass(1, slope, (1.0, 1.0), SLOTS - 1, SLOTS)

    for side in range(2):
        wait(side, rho_copies[side : side + 1])

    candidates = jnp.concatenate([idt[0], idt[1], idt[2]], axis=0)
    wanted = jnp.full((1, LANES), -2, jnp.int32)
    lane1 = iota((1, LANES), 1)
    spread = jnp.concatenate(
        [nbr_mat[...], jnp.zeros((SLOTS, LANES - NBR), jnp.int32)], axis=1
    )
    for s in range(SLOTS):
        line = spread[s : s + 1]
        if s:
            line = pltpu.roll(line, s * PAD, 1)
        wanted = jnp.where((lane1 >= s * PAD) & (lane1 < s * PAD + NBR), line, wanted)
    match = (candidates == wanted.astype(F32)).astype(F32)
    match = jnp.transpose(jnp.concatenate([match, jnp.zeros((104, LANES), F32)], axis=0))
    news = jnp.concatenate([rho[0], rho[1], rho[2], jnp.zeros((104, LANES), F32)], axis=0)
    patch = exact(match.astype(BF16), news)
    hits = jnp.sum(match, axis=1, keepdims=True)
    dens = jnp.where(hits > 0.5, patch, field(6))
    inv5 = inv2 * inv2 * inv_len
    front = field(5) * jnp.exp(jnp.log(dens) * (-1.0 / 3.0)) * inv5
    factor = mass * front
    put_m([factor * x[0], factor * x[1], factor * x[2], factor])

    other_force = pair_pass(2, slope, (1.0, 1.0))

    for s in range(SLOTS):
        result = mid(front, s) * sums_of(own_force[s], own_x[s])
        result = (6.0 * NORM) * (result + sums_of(other_force[s], own_x[s]))
        o_acc[:, s, :] = jnp.where(s < cnt[0], result, 0.0)[0:3]

    for copy in second_stage:
        copy.wait()
    o_arr[...] = st3[...]


def finish(n_gx, n_gy, den, news, acc, rows, o_den, o_acc, o_arr):
    base = (lax.axis_index("gx") * n_gy + lax.axis_index("gy")) * CELLS
    row_id = (iota((CELLS, LANES), 0) + base).astype(F32)
    table = den[...]
    for s in range(SLOTS):
        table = jnp.where(row_id == news[8 + s : 9 + s, :], news[s : s + 1, :], table)
    o_den[...] = table
    o_acc[...] = acc[...]
    turned = jnp.transpose(rows[...])
    halves = jnp.concatenate([turned[0:8], turned[8:16]], axis=1)
    width = 2 * n_gx * n_gy
    source = iota((2 * LANES, width), 0)
    column = iota((2 * LANES, width), 1)
    spot = (source % LANES) * 2 + source // LANES
    spread = (spot == column).astype(F32).astype(BF16)
    o_arr[...] = exact_rows(halves, spread)[0:7]


def exact_rows(value, select):
    return sum(dot(part.astype(BF16), select) for part in parts(value, 3))


def sums_of(total, own_x):
    return own_x * total[3:4] - total


def local(
    n_gx,
    n_gy,
    positions,
    masses,
    smoothing,
    entropy,
    density,
    active_cells,
    active_count,
    neighbours,
    mig_source,
    mig_dest,
):
    vmem = pl.BlockSpec(memory_space=pltpu.VMEM)
    hbm = pl.BlockSpec(memory_space=pl.ANY)
    n_dev = n_gx * n_gy
    entries = SLOTS * PAD
    dma = pltpu.SemaphoreType.DMA
    keep = functools.partial(pltpu.with_memory_space_constraint, memory_space=pltpu.HBM)
    rho, acc, rows = pl.pallas_call(
        functools.partial(kernel, n_gx, n_gy),
        out_shape=(
            jax.ShapeDtypeStruct((16, LANES), F32),
            jax.ShapeDtypeStruct((3, SLOTS, LANES), F32),
            jax.ShapeDtypeStruct((LANES, LANES), F32),
        ),
        in_specs=[hbm] * 11,
        out_specs=(vmem, vmem, vmem),
        scratch_shapes=[
            pltpu.SMEM((SLOTS,), jnp.int32),
            pltpu.SMEM((1,), jnp.int32),
            pltpu.SMEM((SLOTS, NBR), jnp.int32),
            pltpu.SMEM((ROWS,), jnp.int32),
            pltpu.VMEM((1, ROWS), jnp.int32),
            pltpu.VMEM((1, ROWS), jnp.int32),
            pltpu.VMEM((SLOTS, NBR), jnp.int32),
            pltpu.VMEM((8 * CELLS, LANES), F32),
            pltpu.VMEM((4 * EXT, LANES), F32),
            pltpu.VMEM((4 * EXT, LANES), F32),
            pltpu.VMEM((entries * 4, LANES), F32),
            pltpu.VMEM((entries * 4, LANES), F32),
            pltpu.VMEM((2 * entries * 24, LANES), F32),
            pltpu.VMEM((entries * 16, LANES), F32),
            pltpu.VMEM((2 * SLOTS, LANES, LANES), BF16),
            pltpu.VMEM((NBR * LANES, LANES), F32),
            pltpu.VMEM((NBR * LANES, LANES), BF16),
            pltpu.VMEM((NBR * LANES, LANES), BF16),
            pltpu.VMEM((SLOTS, 8, LANES), F32),
            pltpu.VMEM((3, 8, LANES), F32),
            pltpu.VMEM((3, 8, LANES), F32),
            pltpu.VMEM((LANES, LANES), F32),
            pltpu.VMEM((LANES, LANES), F32),
            pltpu.VMEM((LANES, LANES), F32),
            pltpu.VMEM((LANES, LANES), F32),
            dma((7,)),
            dma((2, 7)),
            dma((2, 7)),
            dma((2, 7)),
            dma((2,)),
            dma((2,)),
            dma((2,)),
            dma((2,)),
            dma((n_gy,)),
            dma((n_gy,)),
            dma((n_gx,)),
            dma((n_gx,)),
        ],
        compiler_params=pltpu.CompilerParams(
            collective_id=0, has_side_effects=True, vmem_limit_bytes=16 << 20
        ),
    )(
        keep(active_cells),
        active_count,
        keep(neighbours),
        keep(mig_source),
        keep(positions),
        keep(masses),
        keep(smoothing),
        keep(entropy),
        keep(density),
        keep(mig_source.reshape(1, ROWS)),
        keep(mig_dest.reshape(1, ROWS)),
    )
    return pl.pallas_call(
        functools.partial(finish, n_gx, n_gy),
        out_shape=(
            jax.ShapeDtypeStruct((CELLS, LANES), F32),
            jax.ShapeDtypeStruct((3, SLOTS, LANES), F32),
            jax.ShapeDtypeStruct((7, 2 * n_dev), F32),
        ),
        in_specs=[vmem] * 4,
        out_specs=(vmem, vmem, vmem),
        compiler_params=pltpu.CompilerParams(vmem_limit_bytes=4 << 20),
    )(density, rho, acc, rows)


def solution(mesh):
    both = ("gx", "gy")
    placed = (
        P(None, both, None),
        P(both, None),
        P(both, None),
        P(both, None),
        P(both, None),
        P(both),
        P(both),
        P(both, None),
        P(both),
        P(both, None),
    )
    return jax.shard_map(
        functools.partial(local, mesh.shape["gx"], mesh.shape["gy"]),
        mesh=mesh,
        in_specs=placed,
        out_specs=(P(both, None), P(None, both, None), P(None, both)),
        check_vma=False,
    )
```

```python
import functools
import math

import jax
import jax.numpy as jnp
from jax import lax
from jax.experimental import pallas as pl
from jax.experimental.pallas import tpu as pltpu
from jax.sharding import PartitionSpec as P

CELLS = 256
LANES = 128
RIM = 64
EXT = CELLS + 2 * RIM
NBR = 27
PAD = 32
SLOTS = 4
ROWS = 128
NORM = 8.0 / math.pi
TINY = 1e-12
CHUNK = 32

F32 = jnp.float32
BF16 = jnp.bfloat16
MESH = pl.DeviceIdType.MESH
NT = (((1,), (1,)), ((), ()))
NN = (((1,), (0,)), ((), ()))


def dot(a, b, dims=NN):
    return lax.dot_general(a, b, dims, preferred_element_type=F32)


def parts(value, count):
    out = []
    for _ in range(count - 1):
        head = value.astype(BF16).astype(F32)
        out.append(head)
        value = value - head
    out.append(value.astype(BF16).astype(F32))
    return out


def exact(select, value, dims=NN):
    return sum(dot(select, part.astype(BF16), dims) for part in parts(value, 3))


def iota(shape, dim):
    return lax.broadcasted_iota(jnp.int32, shape, dim)


def kernel(
    n_gx,
    n_gy,
    act_h,
    cnt_h,
    nbr_h,
    src_h,
    pos,
    mas,
    smo,
    ent,
    den,
    src_row_h,
    dst_row_h,
    o_rho,
    o_acc,
    o_arr,
    act,
    cnt,
    nbr,
    src,
    src_row,
    dst_row,
    nbr_mat,
    own,
    ext,
    ext2,
    tiles,
    tiles2,
    bpart,
    mtile,
    ab,
    sq,
    hi_part,
    lo_part,
    acc,
    idt,
    rho,
    outb,
    st1,
    st2,
    st3,
    small_sem,
    load_sem,
    rim_send,
    rim_recv,
    id_send,
    id_recv,
    rho_send,
    rho_recv,
    a_send,
    a_recv,
    b_send,
    b_recv,
):
    gx, gy = lax.axis_index("gx"), lax.axis_index("gy")
    n_dev = n_gx * n_gy
    me = gx * n_gy + gy
    prev, nxt = (me + n_dev - 1) % n_dev, (me + 1) % n_dev
    near = [(prev // n_gy, prev % n_gy), (nxt // n_gy, nxt % n_gy)]

    has = [me > 0, me < n_dev - 1]

    def start(side, copies):
        @pl.when(has[side])
        def _():
            for copy in copies:
                copy.start()

    def wait(side, copies):
        @pl.when(has[side])
        def _():
            for copy in copies:
                copy.wait_send()

        @pl.when(has[1 - side])
        def _():
            for copy in copies:
                copy.wait_recv()

    for at in (1, 2):
        idt[at] = jnp.full((8, LANES), -1.0, F32)
        rho[at] = jnp.ones((8, LANES), F32)

    barrier = pltpu.get_barrier_semaphore()
    for target in near:
        pl.semaphore_signal(barrier, inc=1, device_id=target, device_id_type=MESH)
    for k in range(1, n_gy):
        pl.semaphore_signal(
            barrier, inc=1, device_id=(gx, (gy + k) % n_gy), device_id_type=MESH
        )
    for k in range(1, n_gx):
        pl.semaphore_signal(
            barrier, inc=1, device_id=((gx + k) % n_gx, gy), device_id_type=MESH
        )

    fields = [pos.at[0], pos.at[1], pos.at[2], mas, smo, ent, den]

    def place_of(v, row, rows):
        if v < 4:
            return ext.at[pl.ds(v * EXT + row, rows)]
        return ext2.at[pl.ds((v - 4) * EXT + row, rows)]

    loads = [
        pltpu.make_async_copy(f, own.at[pl.ds(v * CELLS, CELLS)], load_sem.at[0, v])
        for v, f in enumerate(fields)
    ]
    fills = [
        pltpu.make_async_copy(f, place_of(v, RIM, CELLS), load_sem.at[1, v])
        for v, f in enumerate(fields)
    ]
    small = [
        pltpu.make_async_copy(a, b, small_sem.at[i])
        for i, (a, b) in enumerate(
            [
                (act_h, act),
                (cnt_h, cnt),
                (dst_row_h, dst_row),
                (src_row_h, src_row),
                (src_h, src),
                (nbr_h, nbr),
                (nbr_h, nbr_mat),
            ]
        )
    ]
    for copy in small + loads + fills:
        copy.start()
    pl.semaphore_wait(barrier, 2 + n_gy - 1 + n_gx - 1)
    def rim(side, v):
        first = 0 if side == 0 else CELLS - RIM
        land = RIM + CELLS if side == 0 else 0
        return pltpu.make_async_remote_copy(
            src_ref=fields[v].at[pl.ds(first, RIM)],
            dst_ref=place_of(v, land, RIM),
            send_sem=rim_send.at[side, v],
            recv_sem=rim_recv.at[side, v],
            device_id=near[side],
            device_id_type=MESH,
        )

    early = [[rim(side, v) for v in range(4)] for side in range(2)]
    late = [[rim(side, v) for v in range(4, 7)] for side in range(2)]
    for side, target in enumerate(near):
        late[side].append(
            pltpu.make_async_remote_copy(
                src_ref=idt.at[0],
                dst_ref=idt.at[2 - side],
                send_sem=id_send.at[side],
                recv_sem=id_recv.at[side],
                device_id=target,
                device_id_type=MESH,
            )
        )
    for side in range(2):
        start(side, early[side])
    for copy in small:
        copy.wait()

    base = me * CELLS
    sub8 = iota((8, LANES), 0)
    ids = jnp.full((8, LANES), -1, jnp.int32)
    for s in range(SLOTS):
        ids = jnp.where((sub8 == s) & (s < cnt[0]), act[s], ids)
    idt[0] = ids.astype(F32)
    ext2[pl.ds(3 * EXT, EXT), :] = jnp.zeros((EXT, LANES), F32)
    own[pl.ds(7 * CELLS, CELLS), :] = jnp.zeros((CELLS, LANES), F32)

    dest = dst_row[...]
    place = (dest % n_gy) * n_gx + dest // n_gy
    to_dest = (iota((LANES, ROWS), 0) == place).astype(F32)
    earlier = (iota((ROWS, ROWS), 0) < iota((ROWS, ROWS), 1)).astype(F32)
    before = dot(to_dest.astype(BF16), earlier.astype(BF16))
    rank = jnp.sum(to_dest * before, axis=0, keepdims=True)
    to_dest = to_dest.astype(BF16)
    src_cell = src_row[...] // LANES
    src_lane = src_row[...] % LANES
    pick_lane = (iota((LANES, ROWS), 0) == src_lane).astype(F32).astype(BF16)
    from_slot = ((src_cell + base).astype(F32) == idt[0]).astype(F32)
    is_new = jnp.sum(from_slot, axis=0, keepdims=True)

    wanted = jnp.full((1, LANES), -2, jnp.int32)
    lane1 = iota((1, LANES), 1)
    spread = jnp.concatenate(
        [nbr_mat[...], jnp.zeros((SLOTS, LANES - NBR), jnp.int32)], axis=1
    )
    for s in range(SLOTS):
        line = spread[s : s + 1]
        if s:
            line = pltpu.roll(line, s * PAD, 1)
        wanted = jnp.where((lane1 >= s * PAD) & (lane1 < s * PAD + NBR), line, wanted)

    for copy in loads:
        copy.wait()

    lane8 = iota((8, LANES), 1)

    def mig_row(r, state):
        where_from = src[r]
        tile = own[pl.ds(where_from // LANES, 8, stride=CELLS), :]
        value = jnp.sum(
            jnp.where(lane8 == where_from % LANES, tile, 0.0), axis=1, keepdims=True
        )
        return jnp.where(lane8 == r, value, state)

    state = lax.fori_loop(0, ROWS, mig_row, jnp.zeros((8, LANES), F32), unroll=8)
    own_len = []
    for s in range(SLOTS):
        row = jnp.clip(act[s] - base, 0, CELLS - 1)
        own_len.append(own[pl.ds(row + 4 * CELLS, 1), :])
    for s in range(SLOTS):
        for t in (tiles, tiles2):
            t[(s * PAD + NBR) * 4 : (s + 1) * PAD * 4, :] = jnp.ones(
                ((PAD - NBR) * 4, LANES), F32
            )
    bpart[...] = jnp.zeros_like(bpart)
    mtile[...] = jnp.zeros_like(mtile)

    for copy in fills:
        copy.wait()
    for side in range(2):
        wait(side, early[side])
        start(side, late[side])

    def gather(into, out_of):
        for s in range(SLOTS):
            def fetch(k, _, s=s):
                cell = jnp.clip(nbr[s, k] - (base - RIM), 0, EXT - 1)
                into[pl.ds((s * PAD + k) * 4, 4), :] = out_of[pl.ds(cell, 4, stride=EXT), :]
                return 0

            lax.fori_loop(0, NBR, fetch, 0, unroll=9)

    entries = SLOTS * PAD
    gather(tiles, ext)
    k_of = iota((entries, LANES), 0) % PAD
    offset = [k_of // 9 - 1, (k_of // 3) % 3 - 1, k_of % 3 - 1]

    def field(v):
        ref = tiles if v < 4 else tiles2
        return ref[pl.ds(v % 4, entries, stride=4), :]

    x = [field(v) - 0.5 + offset[v].astype(F32) for v in range(3)]
    mass = field(3)
    n2 = x[0] * x[0] + x[1] * x[1] + x[2] * x[2]

    def put_b(at, values):
        for c, value in enumerate(values):
            for p, part in enumerate(parts(value, 3)):
                bpart[pl.ds(at * entries * 24 + p * 8 + c, entries, stride=24), :] = part

    def put_m(values):
        for c, value in enumerate(values):
            for p, part in enumerate(parts(value, 2)):
                mtile[pl.ds(p * 8 + c, entries, stride=16), :] = part

    one = jnp.ones((entries, LANES), F32)
    put_b(0, [x[0], x[1], x[2], n2, one])
    put_m([mass * x[0], mass * x[1], mass * x[2], mass])

    def mid(value, s):
        return value[s * PAD + NBR // 2 : s * PAD + NBR // 2 + 1, :]

    own_x, own_inv = [], []
    zero3 = jnp.zeros((3, LANES), F32)
    for s in range(SLOTS):
        xs = [mid(x[v], s) for v in range(3)]
        inv = 1.0 / own_len[s]
        hi2, ns = inv * inv, mid(n2, s)
        own_x.append(jnp.concatenate(xs + [jnp.zeros((5, LANES), F32)], axis=0))
        own_inv.append(inv)
        scaled = jnp.concatenate([-2.0 * hi2 * v for v in xs] + [hi2, hi2 * ns, zero3], axis=0)
        plain = jnp.concatenate(
            [-2.0 * v for v in xs] + [jnp.ones((1, LANES), F32), ns, zero3], axis=0
        )
        for at, tile in ((s, scaled), (SLOTS + s, plain)):
            h, m, l = parts(tile, 3)
            big = jnp.concatenate([h, h, m, m, h, l, jnp.zeros((80, LANES), F32)], axis=0)
            ab[at] = jnp.transpose(big).astype(BF16)

    def make(step, k):
        a_at = jnp.where(step < SLOTS, step, step - SLOTS)
        b_at = jnp.where(step < 2 * SLOTS, step % SLOTS, step - SLOTS) * PAD
        t = bpart[pl.ds(pl.multiple_of((b_at + k) * 24, 8), 24), :]
        h, m, l = t[0:8], t[8:16], t[16:24]
        b = jnp.concatenate([h, m, h, m, l, h], axis=0).astype(BF16)
        sq[k * LANES : (k + 1) * LANES, :] = dot(ab[a_at][:, :48], b)

    def pair_pass(number, function, signs, first=0, last=SLOTS):
        def slot(s, _):
            after = jnp.minimum(number * SLOTS + s + 1, 3 * SLOTS - 1)
            total = jnp.zeros((16, LANES), F32)

            def work(k):
                for r in range(k * LANES, (k + 1) * LANES, CHUNK):
                    rows = slice(r, r + CHUNK)
                    hi_part[rows, :], lo_part[rows, :] = function(
                        jnp.maximum(sq[rows, :], TINY)
                    )

            def reduce(k):
                e = s * PAD + k
                rows = slice(k * LANES, (k + 1) * LANES)
                lhs = mtile[pl.ds(pl.multiple_of(e * 16, 16), 16), :]
                lhs = jnp.concatenate([lhs if f == 1.0 else lhs * f for f in signs], axis=1).astype(BF16)
                return dot(
                    lhs, jnp.concatenate([hi_part[rows, :], lo_part[rows, :]], axis=1), NT
                )

            for k in range(NBR):
                work(k)
                if k:
                    total = total + reduce(k - 1)
                    make(after, k - 1)
            total = total + reduce(NBR - 1)
            make(after, NBR - 1)
            acc[s] = total[0:8] + total[8:16]
            return 0

        lax.fori_loop(first, last, slot, 0, unroll=True)
        return [acc[s] for s in range(SLOTS)]

    def weight(q2):
        q = q2 * lax.rsqrt(q2)
        u = jnp.maximum(1.0 - q, 0.0)
        v = jnp.maximum(u - q, 0.0)
        return (u * u * u).astype(BF16), (v * v * v).astype(BF16)

    def slope(q2):
        inv_q = lax.rsqrt(q2)
        q = q2 * inv_q
        g = jnp.clip(inv_q, 1.0, 2.0) + jnp.maximum(-3.0 * q, jnp.minimum(q - 2.0, -1.0))
        high = g.astype(BF16)
        return high, (g - high.astype(F32)).astype(BF16)

    for k in range(NBR):
        make(0, k)
    sums = pair_pass(0, weight, (2.0, -1.0))
    rho_rows = []
    for s in range(SLOTS):
        rho_rows.append(NORM * sums[s][3:4] * own_inv[s] * own_inv[s] * own_inv[s])
    rho8 = jnp.concatenate(rho_rows + [jnp.ones((4, LANES), F32)], axis=0)
    rho[0] = rho8

    moved = jnp.sum(from_slot * exact_rows(rho8, pick_lane), axis=0, keepdims=True)
    fresh = jnp.where(is_new > 0.5, moved, state[6:7])
    full = jnp.where(sub8 == 6, fresh, state)
    ranked = jnp.concatenate(
        [
            jnp.where(rank < 0.5, full, 0.0),
            jnp.where(rank < 0.5, 0.0, full),
            jnp.zeros((112, LANES), F32),
        ],
        axis=0,
    )
    outb[...] = exact(to_dest, ranked, NT)

    rho_copies = [
        pltpu.make_async_remote_copy(
            src_ref=rho.at[0],
            dst_ref=rho.at[2 - side],
            send_sem=rho_send.at[side],
            recv_sem=rho_recv.at[side],
            device_id=target,
            device_id_type=MESH,
        )
        for side, target in enumerate(near)
    ]
    first_stage = []
    for k in range(1, n_gy):
        other = (gy + k) % n_gy
        first_stage.append(
            pltpu.make_async_remote_copy(
                src_ref=outb.at[pl.ds(pl.multiple_of(other * n_gx, n_gx), n_gx)],
                dst_ref=st1.at[pl.ds(pl.multiple_of(gy * n_gx, n_gx), n_gx)],
                send_sem=a_send.at[k],
                recv_sem=a_recv.at[k],
                device_id=(gx, other),
                device_id_type=MESH,
            )
        )
    for side in range(2):
        start(side, rho_copies[side : side + 1])
    for copy in first_stage:
        copy.start()
    mine = pl.ds(pl.multiple_of(gy * n_gx, n_gx), n_gx)
    st1[mine, :] = outb[mine, :]
    o_rho[0:8, :] = rho8
    o_rho[8:16, :] = idt[0]

    for side in range(2):
        wait(side, late[side])
    gather(tiles2, ext2)
    inv_len = 1.0 / field(4)
    inv2 = inv_len * inv_len
    put_b(1, [x[0] * inv2, x[1] * inv2, x[2] * inv2, n2 * inv2, inv2])

    pair_pass(1, slope, (1.0, 1.0), 0, SLOTS - 1)

    for copy in first_stage:
        copy.wait()
    for a in range(n_gx):
        st2[a * n_gy : (a + 1) * n_gy, :] = st1[pl.ds(a, n_gy, stride=n_gx), :]
    second_stage = []
    for k in range(1, n_gx):
        other = (gx + k) % n_gx
        second_stage.append(
            pltpu.make_async_remote_copy(
                src_ref=st2.at[pl.ds(pl.multiple_of(other * n_gy, n_gy), n_gy)],
                dst_ref=st3.at[pl.ds(pl.multiple_of(gx * n_gy, n_gy), n_gy)],
                send_sem=b_send.at[k],
                recv_sem=b_recv.at[k],
                device_id=(other, gy),
                device_id_type=MESH,
            )
        )
    for copy in second_stage:
        copy.start()
    mine = pl.ds(pl.multiple_of(gx * n_gy, n_gy), n_gy)
    st3[mine, :] = st2[mine, :]
    own_force = pair_pass(1, slope, (1.0, 1.0), SLOTS - 1, SLOTS)

    for side in range(2):
        wait(side, rho_copies[side : side + 1])

    candidates = jnp.concatenate([idt[0], idt[1], idt[2]], axis=0)
    match = (candidates == wanted.astype(F32)).astype(F32)
    match = jnp.transpose(jnp.concatenate([match, jnp.zeros((104, LANES), F32)], axis=0))
    news = jnp.concatenate([rho[0], rho[1], rho[2], jnp.zeros((104, LANES), F32)], axis=0)
    patch = exact(match.astype(BF16), news)
    hits = jnp.sum(match, axis=1, keepdims=True)
    dens = jnp.where(hits > 0.5, patch, field(6))
    inv5 = inv2 * inv2 * inv_len
    front = field(5) * jnp.exp(jnp.log(dens) * (-1.0 / 3.0)) * inv5
    factor = mass * front
    put_m([factor * x[0], factor * x[1], factor * x[2], factor])

    other_force = pair_pass(2, slope, (1.0, 1.0))

    for s in range(SLOTS):
        result = mid(front, s) * sums_of(own_force[s], own_x[s])
        result = (6.0 * NORM) * (result + sums_of(other_force[s], own_x[s]))
        o_acc[:, s, :] = jnp.where(s < cnt[0], result, 0.0)[0:3]

    for copy in second_stage:
        copy.wait()
    o_arr[...] = st3[...]


def finish(n_gx, n_gy, den, news, acc, rows, o_den, o_acc, o_arr):
    base = (lax.axis_index("gx") * n_gy + lax.axis_index("gy")) * CELLS
    row_id = (iota((CELLS, LANES), 0) + base).astype(F32)
    table = den[...]
    for s in range(SLOTS):
        table = jnp.where(row_id == news[8 + s : 9 + s, :], news[s : s + 1, :], table)
    o_den[...] = table
    o_acc[...] = acc[...]
    turned = jnp.transpose(rows[...])
    halves = jnp.concatenate([turned[0:8], turned[8:16]], axis=1)
    width = 2 * n_gx * n_gy
    source = iota((2 * LANES, width), 0)
    column = iota((2 * LANES, width), 1)
    spot = (source % LANES) * 2 + source // LANES
    spread = (spot == column).astype(F32).astype(BF16)
    o_arr[...] = exact_rows(halves, spread)[0:7]


def exact_rows(value, select):
    return sum(dot(part.astype(BF16), select) for part in parts(value, 3))


def sums_of(total, own_x):
    return own_x * total[3:4] - total


def local(
    n_gx,
    n_gy,
    positions,
    masses,
    smoothing,
    entropy,
    density,
    active_cells,
    active_count,
    neighbours,
    mig_source,
    mig_dest,
):
    vmem = pl.BlockSpec(memory_space=pltpu.VMEM)
    hbm = pl.BlockSpec(memory_space=pl.ANY)
    n_dev = n_gx * n_gy
    entries = SLOTS * PAD
    dma = pltpu.SemaphoreType.DMA
    keep = functools.partial(pltpu.with_memory_space_constraint, memory_space=pltpu.HBM)
    rho, acc, rows = pl.pallas_call(
        functools.partial(kernel, n_gx, n_gy),
        out_shape=(
            jax.ShapeDtypeStruct((16, LANES), F32),
            jax.ShapeDtypeStruct((3, SLOTS, LANES), F32),
            jax.ShapeDtypeStruct((LANES, LANES), F32),
        ),
        in_specs=[hbm] * 11,
        out_specs=(vmem, vmem, vmem),
        scratch_shapes=[
            pltpu.SMEM((SLOTS,), jnp.int32),
            pltpu.SMEM((1,), jnp.int32),
            pltpu.SMEM((SLOTS, NBR), jnp.int32),
            pltpu.SMEM((ROWS,), jnp.int32),
            pltpu.VMEM((1, ROWS), jnp.int32),
            pltpu.VMEM((1, ROWS), jnp.int32),
            pltpu.VMEM((SLOTS, NBR), jnp.int32),
            pltpu.VMEM((8 * CELLS, LANES), F32),
            pltpu.VMEM((4 * EXT, LANES), F32),
            pltpu.VMEM((4 * EXT, LANES), F32),
            pltpu.VMEM((entries * 4, LANES), F32),
            pltpu.VMEM((entries * 4, LANES), F32),
            pltpu.VMEM((2 * entries * 24, LANES), F32),
            pltpu.VMEM((entries * 16, LANES), F32),
            pltpu.VMEM((2 * SLOTS, LANES, LANES), BF16),
            pltpu.VMEM((NBR * LANES, LANES), F32),
            pltpu.VMEM((NBR * LANES, LANES), BF16),
            pltpu.VMEM((NBR * LANES, LANES), BF16),
            pltpu.VMEM((SLOTS, 8, LANES), F32),
            pltpu.VMEM((3, 8, LANES), F32),
            pltpu.VMEM((3, 8, LANES), F32),
            pltpu.VMEM((LANES, LANES), F32),
            pltpu.VMEM((LANES, LANES), F32),
            pltpu.VMEM((LANES, LANES), F32),
            pltpu.VMEM((LANES, LANES), F32),
            dma((7,)),
            dma((2, 7)),
            dma((2, 7)),
            dma((2, 7)),
            dma((2,)),
            dma((2,)),
            dma((2,)),
            dma((2,)),
            dma((n_gy,)),
            dma((n_gy,)),
            dma((n_gx,)),
            dma((n_gx,)),
        ],
        compiler_params=pltpu.CompilerParams(
            collective_id=0, has_side_effects=True, vmem_limit_bytes=16 << 20
        ),
    )(
        keep(active_cells),
        active_count,
        keep(neighbours),
        keep(mig_source),
        keep(positions),
        keep(masses),
        keep(smoothing),
        keep(entropy),
        keep(density),
        keep(mig_source.reshape(1, ROWS)),
        keep(mig_dest.reshape(1, ROWS)),
    )
    return pl.pallas_call(
        functools.partial(finish, n_gx, n_gy),
        out_shape=(
            jax.ShapeDtypeStruct((CELLS, LANES), F32),
            jax.ShapeDtypeStruct((3, SLOTS, LANES), F32),
            jax.ShapeDtypeStruct((7, 2 * n_dev), F32),
        ),
        in_specs=[vmem] * 4,
        out_specs=(vmem, vmem, vmem),
        compiler_params=pltpu.CompilerParams(vmem_limit_bytes=4 << 20),
    )(density, rho, acc, rows)


def solution(mesh):
    both = ("gx", "gy")
    placed = (
        P(None, both, None),
        P(both, None),
        P(both, None),
        P(both, None),
        P(both, None),
        P(both),
        P(both),
        P(both, None),
        P(both),
        P(both, None),
    )
    return jax.shard_map(
        functools.partial(local, mesh.shape["gx"], mesh.shape["gy"]),
        mesh=mesh,
        in_specs=placed,
        out_specs=(P(both, None), P(None, both, None), P(None, both)),
        check_vma=False,
    )
```

```python
import functools
import math

import jax
import jax.numpy as jnp
from jax import lax
from jax.experimental import pallas as pl
from jax.experimental.pallas import tpu as pltpu
from jax.sharding import PartitionSpec as P

CELLS = 256
LANES = 128
RIM = 64
EXT = CELLS + 2 * RIM
NBR = 27
PAD = 32
SLOTS = 4
ROWS = 128
NORM = 8.0 / math.pi
TINY = 1e-12
CHUNK = 32

F32 = jnp.float32
BF16 = jnp.bfloat16
MESH = pl.DeviceIdType.MESH
NT = (((1,), (1,)), ((), ()))
NN = (((1,), (0,)), ((), ()))


def dot(a, b, dims=NN):
    return lax.dot_general(a, b, dims, preferred_element_type=F32)


def parts(value, count):
    out = []
    for _ in range(count - 1):
        head = value.astype(BF16).astype(F32)
        out.append(head)
        value = value - head
    out.append(value.astype(BF16).astype(F32))
    return out


def exact(select, value, dims=NN):
    return sum(dot(select, part.astype(BF16), dims) for part in parts(value, 3))


def iota(shape, dim):
    return lax.broadcasted_iota(jnp.int32, shape, dim)


def kernel(
    n_gx,
    n_gy,
    act_h,
    cnt_h,
    nbr_h,
    src_h,
    pos,
    mas,
    smo,
    ent,
    den,
    src_row_h,
    dst_row_h,
    o_rho,
    o_acc,
    o_arr,
    act,
    cnt,
    nbr,
    src,
    src_row,
    dst_row,
    nbr_mat,
    own,
    ext,
    ext2,
    tiles,
    tiles2,
    bpart,
    mtile,
    ab,
    sq,
    hi_part,
    lo_part,
    acc,
    idt,
    rho,
    outb,
    st1,
    st2,
    st3,
    small_sem,
    load_sem,
    rim_send,
    rim_recv,
    id_send,
    id_recv,
    rho_send,
    rho_recv,
    a_send,
    a_recv,
    b_send,
    b_recv,
):
    gx, gy = lax.axis_index("gx"), lax.axis_index("gy")
    n_dev = n_gx * n_gy
    me = gx * n_gy + gy
    prev, nxt = (me + n_dev - 1) % n_dev, (me + 1) % n_dev
    near = [(prev // n_gy, prev % n_gy), (nxt // n_gy, nxt % n_gy)]

    has = [me > 0, me < n_dev - 1]

    def start(side, copies):
        @pl.when(has[side])
        def _():
            for copy in copies:
                copy.start()

    def wait(side, copies):
        @pl.when(has[side])
        def _():
            for copy in copies:
                copy.wait_send()

        @pl.when(has[1 - side])
        def _():
            for copy in copies:
                copy.wait_recv()

    for at in (1, 2):
        idt[at] = jnp.full((8, LANES), -1.0, F32)
        rho[at] = jnp.ones((8, LANES), F32)

    barrier = pltpu.get_barrier_semaphore()
    for k in range(1, n_gx):
        pl.semaphore_signal(
            barrier, inc=1, device_id=((gx + k) % n_gx, gy), device_id_type=MESH
        )
    for target in near:
        pl.semaphore_signal(barrier, inc=1, device_id=target, device_id_type=MESH)
    for k in range(1, n_gy):
        pl.semaphore_signal(
            barrier, inc=1, device_id=(gx, (gy + k) % n_gy), device_id_type=MESH
        )

    fields = [pos.at[0], pos.at[1], pos.at[2], mas, smo, ent, den]

    def place_of(v, row, rows):
        if v < 4:
            return ext.at[pl.ds(v * EXT + row, rows)]
        return ext2.at[pl.ds((v - 4) * EXT + row, rows)]

    loads = [
        pltpu.make_async_copy(f, own.at[pl.ds(v * CELLS, CELLS)], load_sem.at[0, v])
        for v, f in enumerate(fields)
    ]
    fills = [
        pltpu.make_async_copy(f, place_of(v, RIM, CELLS), load_sem.at[1, v])
        for v, f in enumerate(fields)
    ]
    small = [
        pltpu.make_async_copy(a, b, small_sem.at[i])
        for i, (a, b) in enumerate(
            [
                (act_h, act),
                (cnt_h, cnt),
                (dst_row_h, dst_row),
                (src_row_h, src_row),
                (src_h, src),
                (nbr_h, nbr),
                (nbr_h, nbr_mat),
            ]
        )
    ]
    for copy in small + loads + fills:
        copy.start()
    pl.semaphore_wait(barrier, 2 + n_gy - 1 + n_gx - 1)
    def rim(side, v):
        first = 0 if side == 0 else CELLS - RIM
        land = RIM + CELLS if side == 0 else 0
        return pltpu.make_async_remote_copy(
            src_ref=fields[v].at[pl.ds(first, RIM)],
            dst_ref=place_of(v, land, RIM),
            send_sem=rim_send.at[side, v],
            recv_sem=rim_recv.at[side, v],
            device_id=near[side],
            device_id_type=MESH,
        )

    early = [[rim(side, v) for v in range(4)] for side in range(2)]
    late = [[rim(side, v) for v in range(4, 7)] for side in range(2)]
    for side, target in enumerate(near):
        late[side].append(
            pltpu.make_async_remote_copy(
                src_ref=idt.at[0],
                dst_ref=idt.at[2 - side],
                send_sem=id_send.at[side],
                recv_sem=id_recv.at[side],
                device_id=target,
                device_id_type=MESH,
            )
        )
    for side in range(2):
        start(side, early[side])
    for copy in small:
        copy.wait()

    base = me * CELLS
    sub8 = iota((8, LANES), 0)
    ids = jnp.full((8, LANES), -1, jnp.int32)
    for s in range(SLOTS):
        ids = jnp.where((sub8 == s) & (s < cnt[0]), act[s], ids)
    idt[0] = ids.astype(F32)
    ext2[pl.ds(3 * EXT, EXT), :] = jnp.zeros((EXT, LANES), F32)
    own[pl.ds(7 * CELLS, CELLS), :] = jnp.zeros((CELLS, LANES), F32)

    dest = dst_row[...]
    place = (dest % n_gy) * n_gx + dest // n_gy
    to_dest = (iota((LANES, ROWS), 0) == place).astype(F32)
    earlier = (iota((ROWS, ROWS), 0) < iota((ROWS, ROWS), 1)).astype(F32)
    before = dot(to_dest.astype(BF16), earlier.astype(BF16))
    rank = jnp.sum(to_dest * before, axis=0, keepdims=True)
    to_dest = to_dest.astype(BF16)
    src_cell = src_row[...] // LANES
    src_lane = src_row[...] % LANES
    pick_lane = (iota((LANES, ROWS), 0) == src_lane).astype(F32).astype(BF16)
    from_slot = ((src_cell + base).astype(F32) == idt[0]).astype(F32)
    is_new = jnp.sum(from_slot, axis=0, keepdims=True)

    wanted = jnp.full((1, LANES), -2, jnp.int32)
    lane1 = iota((1, LANES), 1)
    spread = jnp.concatenate(
        [nbr_mat[...], jnp.zeros((SLOTS, LANES - NBR), jnp.int32)], axis=1
    )
    for s in range(SLOTS):
        line = spread[s : s + 1]
        if s:
            line = pltpu.roll(line, s * PAD, 1)
        wanted = jnp.where((lane1 >= s * PAD) & (lane1 < s * PAD + NBR), line, wanted)

    for copy in loads:
        copy.wait()

    lane8 = iota((8, LANES), 1)

    def mig_row(r, state):
        where_from = src[r]
        tile = own[pl.ds(where_from // LANES, 8, stride=CELLS), :]
        value = jnp.sum(
            jnp.where(lane8 == where_from % LANES, tile, 0.0), axis=1, keepdims=True
        )
        return jnp.where(lane8 == r, value, state)

    state = lax.fori_loop(0, ROWS, mig_row, jnp.zeros((8, LANES), F32), unroll=8)
    own_len = []
    for s in range(SLOTS):
        row = jnp.clip(act[s] - base, 0, CELLS - 1)
        own_len.append(own[pl.ds(row + 4 * CELLS, 1), :])
    for s in range(SLOTS):
        for t in (tiles, tiles2):
            t[(s * PAD + NBR) * 4 : (s + 1) * PAD * 4, :] = jnp.ones(
                ((PAD - NBR) * 4, LANES), F32
            )
    bpart[...] = jnp.zeros_like(bpart)
    mtile[...] = jnp.zeros_like(mtile)

    for copy in fills:
        copy.wait()
    for side in range(2):
        wait(side, early[side])
        start(side, late[side])

    def gather(into, out_of):
        for s in range(SLOTS):
            def fetch(k, _, s=s):
                cell = jnp.clip(nbr[s, k] - (base - RIM), 0, EXT - 1)
                into[pl.ds((s * PAD + k) * 4, 4), :] = out_of[pl.ds(cell, 4, stride=EXT), :]
                return 0

            lax.fori_loop(0, NBR, fetch, 0, unroll=9)

    entries = SLOTS * PAD
    gather(tiles, ext)
    k_of = iota((entries, LANES), 0) % PAD
    offset = [k_of // 9 - 1, (k_of // 3) % 3 - 1, k_of % 3 - 1]

    def field(v):
        ref = tiles if v < 4 else tiles2
        return ref[pl.ds(v % 4, entries, stride=4), :]

    x = [field(v) - 0.5 + offset[v].astype(F32) for v in range(3)]
    mass = field(3)
    n2 = x[0] * x[0] + x[1] * x[1] + x[2] * x[2]

    def put_b(at, values):
        for c, value in enumerate(values):
            for p, part in enumerate(parts(value, 3)):
                bpart[pl.ds(at * entries * 24 + p * 8 + c, entries, stride=24), :] = part

    def put_m(values):
        for c, value in enumerate(values):
            for p, part in enumerate(parts(value, 2)):
                mtile[pl.ds(p * 8 + c, entries, stride=16), :] = part

    one = jnp.ones((entries, LANES), F32)
    put_b(0, [x[0], x[1], x[2], n2, one])
    put_m([mass * x[0], mass * x[1], mass * x[2], mass])

    def mid(value, s):
        return value[s * PAD + NBR // 2 : s * PAD + NBR // 2 + 1, :]

    own_x, own_inv = [], []
    zero3 = jnp.zeros((3, LANES), F32)
    for s in range(SLOTS):
        xs = [mid(x[v], s) for v in range(3)]
        inv = 1.0 / own_len[s]
        hi2, ns = inv * inv, mid(n2, s)
        own_x.append(jnp.concatenate(xs + [jnp.zeros((5, LANES), F32)], axis=0))
        own_inv.append(inv)
        scaled = jnp.concatenate([-2.0 * hi2 * v for v in xs] + [hi2, hi2 * ns, zero3], axis=0)
        plain = jnp.concatenate(
            [-2.0 * v for v in xs] + [jnp.ones((1, LANES), F32), ns, zero3], axis=0
        )
        for at, tile in ((s, scaled), (SLOTS + s, plain)):
            h, m, l = parts(tile, 3)
            big = jnp.concatenate([h, h, m, m, h, l, jnp.zeros((80, LANES), F32)], axis=0)
            ab[at] = jnp.transpose(big).astype(BF16)

    def make(step, k):
        a_at = jnp.where(step < SLOTS, step, step - SLOTS)
        b_at = jnp.where(step < 2 * SLOTS, step % SLOTS, step - SLOTS) * PAD
        t = bpart[pl.ds(pl.multiple_of((b_at + k) * 24, 8), 24), :]
        h, m, l = t[0:8], t[8:16], t[16:24]
        b = jnp.concatenate([h, m, h, m, l, h], axis=0).astype(BF16)
        sq[k * LANES : (k + 1) * LANES, :] = dot(ab[a_at][:, :48], b)

    def pair_pass(number, function, signs, first=0, last=SLOTS):
        def slot(s, _):
            after = jnp.minimum(number * SLOTS + s + 1, 3 * SLOTS - 1)
            total = jnp.zeros((16, LANES), F32)

            def work(k):
                for r in range(k * LANES, (k + 1) * LANES, CHUNK):
                    rows = slice(r, r + CHUNK)
                    hi_part[rows, :], lo_part[rows, :] = function(
                        jnp.maximum(sq[rows, :], TINY)
                    )

            def reduce(k):
                e = s * PAD + k
                rows = slice(k * LANES, (k + 1) * LANES)
                lhs = mtile[pl.ds(pl.multiple_of(e * 16, 16), 16), :]
                lhs = jnp.concatenate([lhs if f == 1.0 else lhs * f for f in signs], axis=1).astype(BF16)
                return dot(
                    lhs, jnp.concatenate([hi_part[rows, :], lo_part[rows, :]], axis=1), NT
                )

            for k in range(NBR):
                work(k)
                if k:
                    total = total + reduce(k - 1)
                    make(after, k - 1)
            total = total + reduce(NBR - 1)
            make(after, NBR - 1)
            acc[s] = total[0:8] + total[8:16]
            return 0

        lax.fori_loop(first, last, slot, 0, unroll=True)
        return [acc[s] for s in range(SLOTS)]

    def weight(q2):
        q = q2 * lax.rsqrt(q2)
        u = jnp.maximum(1.0 - q, 0.0)
        v = jnp.maximum(u - q, 0.0)
        return (u * u * u).astype(BF16), (v * v * v).astype(BF16)

    def slope(q2):
        inv_q = lax.rsqrt(q2)
        q = q2 * inv_q
        g = jnp.clip(inv_q, 1.0, 2.0) + jnp.maximum(-3.0 * q, jnp.minimum(q - 2.0, -1.0))
        high = g.astype(BF16)
        return high, (g - high.astype(F32)).astype(BF16)

    for k in range(NBR):
        make(0, k)
    sums = pair_pass(0, weight, (2.0, -1.0))
    rho_rows = []
    for s in range(SLOTS):
        rho_rows.append(NORM * sums[s][3:4] * own_inv[s] * own_inv[s] * own_inv[s])
    rho8 = jnp.concatenate(rho_rows + [jnp.ones((4, LANES), F32)], axis=0)
    rho[0] = rho8
    rho_copies = [
        pltpu.make_async_remote_copy(
            src_ref=rho.at[0],
            dst_ref=rho.at[2 - side],
            send_sem=rho_send.at[side],
            recv_sem=rho_recv.at[side],
            device_id=target,
            device_id_type=MESH,
        )
        for side, target in enumerate(near)
    ]
    for side in range(2):
        start(side, rho_copies[side : side + 1])

    moved = jnp.sum(from_slot * exact_rows(rho8, pick_lane), axis=0, keepdims=True)
    fresh = jnp.where(is_new > 0.5, moved, state[6:7])
    full = jnp.where(sub8 == 6, fresh, state)
    ranked = jnp.concatenate(
        [
            jnp.where(rank < 0.5, full, 0.0),
            jnp.where(rank < 0.5, 0.0, full),
            jnp.zeros((112, LANES), F32),
        ],
        axis=0,
    )
    outb[...] = exact(to_dest, ranked, NT)

    first_stage = []
    for k in range(1, n_gy):
        other = (gy + k) % n_gy
        first_stage.append(
            pltpu.make_async_remote_copy(
                src_ref=outb.at[pl.ds(pl.multiple_of(other * n_gx, n_gx), n_gx)],
                dst_ref=st1.at[pl.ds(pl.multiple_of(gy * n_gx, n_gx), n_gx)],
                send_sem=a_send.at[k],
                recv_sem=a_recv.at[k],
                device_id=(gx, other),
                device_id_type=MESH,
            )
        )
    for copy in first_stage:
        copy.start()
    mine = pl.ds(pl.multiple_of(gy * n_gx, n_gx), n_gx)
    st1[mine, :] = outb[mine, :]
    o_rho[0:8, :] = rho8
    o_rho[8:16, :] = idt[0]

    for side in range(2):
        wait(side, late[side])
    gather(tiles2, ext2)
    inv_len = 1.0 / field(4)
    inv2 = inv_len * inv_len
    put_b(1, [x[0] * inv2, x[1] * inv2, x[2] * inv2, n2 * inv2, inv2])

    pair_pass(1, slope, (1.0, 1.0), 0, SLOTS - 1)

    for copy in first_stage:
        copy.wait()
    for a in range(n_gx):
        st2[a * n_gy : (a + 1) * n_gy, :] = st1[pl.ds(a, n_gy, stride=n_gx), :]
    second_stage = []
    for k in range(1, n_gx):
        other = (gx + k) % n_gx
        second_stage.append(
            pltpu.make_async_remote_copy(
                src_ref=st2.at[pl.ds(pl.multiple_of(other * n_gy, n_gy), n_gy)],
                dst_ref=st3.at[pl.ds(pl.multiple_of(gx * n_gy, n_gy), n_gy)],
                send_sem=b_send.at[k],
                recv_sem=b_recv.at[k],
                device_id=(other, gy),
                device_id_type=MESH,
            )
        )
    for copy in second_stage:
        copy.start()
    mine = pl.ds(pl.multiple_of(gx * n_gy, n_gy), n_gy)
    st3[mine, :] = st2[mine, :]
    own_force = pair_pass(1, slope, (1.0, 1.0), SLOTS - 1, SLOTS)

    for side in range(2):
        wait(side, rho_copies[side : side + 1])

    candidates = jnp.concatenate([idt[0], idt[1], idt[2]], axis=0)
    match = (candidates == wanted.astype(F32)).astype(F32)
    match = jnp.transpose(jnp.concatenate([match, jnp.zeros((104, LANES), F32)], axis=0))
    news = jnp.concatenate([rho[0], rho[1], rho[2], jnp.zeros((104, LANES), F32)], axis=0)
    patch = exact(match.astype(BF16), news)
    hits = jnp.sum(match, axis=1, keepdims=True)
    dens = jnp.where(hits > 0.5, patch, field(6))
    inv5 = inv2 * inv2 * inv_len
    front = field(5) * jnp.exp(jnp.log(dens) * (-1.0 / 3.0)) * inv5
    factor = mass * front
    put_m([factor * x[0], factor * x[1], factor * x[2], factor])

    other_force = pair_pass(2, slope, (1.0, 1.0))

    for s in range(SLOTS):
        result = mid(front, s) * sums_of(own_force[s], own_x[s])
        result = (6.0 * NORM) * (result + sums_of(other_force[s], own_x[s]))
        o_acc[:, s, :] = jnp.where(s < cnt[0], result, 0.0)[0:3]

    for copy in second_stage:
        copy.wait()
    o_arr[...] = st3[...]


def finish(n_gx, n_gy, den, news, acc, rows, o_den, o_acc, o_arr):
    base = (lax.axis_index("gx") * n_gy + lax.axis_index("gy")) * CELLS
    row_id = (iota((CELLS, LANES), 0) + base).astype(F32)
    table = den[...]
    for s in range(SLOTS):
        table = jnp.where(row_id == news[8 + s : 9 + s, :], news[s : s + 1, :], table)
    o_den[...] = table
    o_acc[...] = acc[...]
    turned = jnp.transpose(rows[...])
    halves = jnp.concatenate([turned[0:8], turned[8:16]], axis=1)
    width = 2 * n_gx * n_gy
    source = iota((2 * LANES, width), 0)
    column = iota((2 * LANES, width), 1)
    spot = (source % LANES) * 2 + source // LANES
    spread = (spot == column).astype(F32).astype(BF16)
    o_arr[...] = exact_rows(halves, spread)[0:7]


def exact_rows(value, select):
    return sum(dot(part.astype(BF16), select) for part in parts(value, 3))


def sums_of(total, own_x):
    return own_x * total[3:4] - total


def local(
    n_gx,
    n_gy,
    positions,
    masses,
    smoothing,
    entropy,
    density,
    active_cells,
    active_count,
    neighbours,
    mig_source,
    mig_dest,
):
    vmem = pl.BlockSpec(memory_space=pltpu.VMEM)
    hbm = pl.BlockSpec(memory_space=pl.ANY)
    n_dev = n_gx * n_gy
    entries = SLOTS * PAD
    dma = pltpu.SemaphoreType.DMA
    keep = functools.partial(pltpu.with_memory_space_constraint, memory_space=pltpu.HBM)
    rho, acc, rows = pl.pallas_call(
        functools.partial(kernel, n_gx, n_gy),
        out_shape=(
            jax.ShapeDtypeStruct((16, LANES), F32),
            jax.ShapeDtypeStruct((3, SLOTS, LANES), F32),
            jax.ShapeDtypeStruct((LANES, LANES), F32),
        ),
        in_specs=[hbm] * 11,
        out_specs=(vmem, vmem, vmem),
        scratch_shapes=[
            pltpu.SMEM((SLOTS,), jnp.int32),
            pltpu.SMEM((1,), jnp.int32),
            pltpu.SMEM((SLOTS, NBR), jnp.int32),
            pltpu.SMEM((ROWS,), jnp.int32),
            pltpu.VMEM((1, ROWS), jnp.int32),
            pltpu.VMEM((1, ROWS), jnp.int32),
            pltpu.VMEM((SLOTS, NBR), jnp.int32),
            pltpu.VMEM((8 * CELLS, LANES), F32),
            pltpu.VMEM((4 * EXT, LANES), F32),
            pltpu.VMEM((4 * EXT, LANES), F32),
            pltpu.VMEM((entries * 4, LANES), F32),
            pltpu.VMEM((entries * 4, LANES), F32),
            pltpu.VMEM((2 * entries * 24, LANES), F32),
            pltpu.VMEM((entries * 16, LANES), F32),
            pltpu.VMEM((2 * SLOTS, LANES, LANES), BF16),
            pltpu.VMEM((NBR * LANES, LANES), F32),
            pltpu.VMEM((NBR * LANES, LANES), BF16),
            pltpu.VMEM((NBR * LANES, LANES), BF16),
            pltpu.VMEM((SLOTS, 8, LANES), F32),
            pltpu.VMEM((3, 8, LANES), F32),
            pltpu.VMEM((3, 8, LANES), F32),
            pltpu.VMEM((LANES, LANES), F32),
            pltpu.VMEM((LANES, LANES), F32),
            pltpu.VMEM((LANES, LANES), F32),
            pltpu.VMEM((LANES, LANES), F32),
            dma((7,)),
            dma((2, 7)),
            dma((2, 7)),
            dma((2, 7)),
            dma((2,)),
            dma((2,)),
            dma((2,)),
            dma((2,)),
            dma((n_gy,)),
            dma((n_gy,)),
            dma((n_gx,)),
            dma((n_gx,)),
        ],
        compiler_params=pltpu.CompilerParams(
            collective_id=0, has_side_effects=True, vmem_limit_bytes=16 << 20
        ),
    )(
        keep(active_cells),
        active_count,
        keep(neighbours),
        keep(mig_source),
        keep(positions),
        keep(masses),
        keep(smoothing),
        keep(entropy),
        keep(density),
        keep(mig_source.reshape(1, ROWS)),
        keep(mig_dest.reshape(1, ROWS)),
    )
    return pl.pallas_call(
        functools.partial(finish, n_gx, n_gy),
        out_shape=(
            jax.ShapeDtypeStruct((CELLS, LANES), F32),
            jax.ShapeDtypeStruct((3, SLOTS, LANES), F32),
            jax.ShapeDtypeStruct((7, 2 * n_dev), F32),
        ),
        in_specs=[vmem] * 4,
        out_specs=(vmem, vmem, vmem),
        compiler_params=pltpu.CompilerParams(vmem_limit_bytes=4 << 20),
    )(density, rho, acc, rows)


def solution(mesh):
    both = ("gx", "gy")
    placed = (
        P(None, both, None),
        P(both, None),
        P(both, None),
        P(both, None),
        P(both, None),
        P(both),
        P(both),
        P(both, None),
        P(both),
        P(both, None),
    )
    return jax.shard_map(
        functools.partial(local, mesh.shape["gx"], mesh.shape["gy"]),
        mesh=mesh,
        in_specs=placed,
        out_specs=(P(both, None), P(None, both, None), P(None, both)),
        check_vma=False,
    )
```
